128 devices in a mesh: section: 16 (over z_hi, y, core), slab: 8 (over x, z_lo).
Axes of the slice: x: 4, y: 4, z: 4 (z_hi: 2, z_lo: 2; z = z_hi * 2 + z_lo), core: 2. Of those that a mesh axis runs over, the one named last changes fastest.
Arguments:
- emitted: bfloat16 [16, 20, 512, 512], P('section', None, 'slab'), may hold values from -6 to 6
- returned: bfloat16 [16, 20, 512, 512], P('section', None, 'slab'), may hold values from -6 to 6
- stash: bfloat16 [16, 20, 512, 512], P('section', None, 'slab'), may hold values from -6 to 6
- skip_w: bfloat16 [16, 2, 20, 20], P('section'), may hold values from -1.25 to 1.25
- up_w: bfloat16 [16, 2, 80, 20], P('section'), may hold values from -1.25 to 1.25
- down_w: bfloat16 [16, 2, 20, 80], P('section'), may hold values from -0.625 to 0.625
- spec_w: bfloat16 [16, 2, 64, 2, 20, 20, 128], P('section', None, 'slab'), may hold values from -4 to 4
Outputs:
- sent: bfloat16 [16, 20, 512, 512], P('section', None, 'slab')
- back_grad: bfloat16 [16, 20, 512, 512], P('section', None, 'slab')
- grad_skip: float32 [16, 2, 20, 20], P('section')
- grad_up: float32 [16, 2, 80, 20], P('section')
- grad_down: float32 [16, 2, 20, 80], P('section')
- grad_spec: float32 [16, 2, 64, 2, 20, 20, 128], P('section', None, 'slab')
The draws below stay inside these ranges and needn't reach their ends.
All inputs are finite; a program needn't handle non-finite values.
Results may differ from the reference program's by a relative error of at most 0.03.
Values may be sent and summed in bfloat16 or wider, within the bound.
No kernel may reach another device: no remote copies, remote signals or barrier semaphores. Data moves between devices by JAX's collectives and lax.ppermute only.
A program may use at most 192 MiB of HBM per device.

```python
import jax
import jax.numpy as jnp
from jax import lax

N = 512
C = 20
F = 80
M = 64
LAYERS = 2
SECTIONS = 16


def block_scale(key, shape, cuts, low, high):
    def one(axis_at, shards_of):
        steps = jax.random.uniform(jax.random.fold_in(jax.random.fold_in(key, 6), axis_at), (shards_of,), jnp.float32, low / len(cuts), high / len(cuts))
        return jnp.repeat(jnp.exp(steps), shape[axis_at] // shards_of).reshape((-1,) + (1,) * (len(shape) - axis_at - 1))

    loudness = one(*cuts[0])
    for cut in cuts[1:]:
        loudness = loudness * one(*cut)
    return loudness


def normal_values(own_key, dims, spread, bound, cuts=(), kind=jnp.bfloat16):
    level = block_scale(own_key, dims, cuts, -0.22, 0.18) if cuts else 1.0
    array = jax.random.normal(own_key, dims, jnp.float32) * spread * level
    return jnp.minimum(jnp.maximum(array, -bound), bound).astype(kind)


def setup_inputs(seed: int = 0) -> dict:
    keys = jax.random.split(jax.random.key(seed), 8)
    return {
        "emitted": normal_values(keys[0], (SECTIONS, C, N, N), 1.0, 6.0, ((0, 16), (2, 8))),
        "returned": normal_values(keys[1], (SECTIONS, C, N, N), 1.0, 6.0, ((0, 16), (2, 8))),
        "stash": normal_values(keys[2], (SECTIONS, C, N, N), 1.0, 6.0, ((0, 16), (2, 8))),
        "skip_w": normal_values(keys[3], (SECTIONS, LAYERS, C, C), C ** -0.5, 1.25, ((0, 16),)),
        "up_w": normal_values(keys[4], (SECTIONS, LAYERS, F, C), C ** -0.5, 1.25, ((0, 16),)),
        "down_w": normal_values(keys[5], (SECTIONS, LAYERS, C, F), F ** -0.5, 0.625, ((0, 16),)),
        "spec_w": normal_values(keys[6], (SECTIONS, LAYERS, M, 2, C, C, 2 * M), 0.6, 4.0, ((0, 16), (2, 8))),
    }


root_two_pi = 0.7978845608028654
cubic_coef = 0.044715


def smooth_gate(values):
    return 0.5 * values * (1.0 + jnp.tanh(root_two_pi * (values + cubic_coef * values * values * values)))


def gate_slope(values):
    tangent = jnp.tanh(root_two_pi * (values + cubic_coef * values * values * values))
    return 0.5 * (1.0 + tangent) + 0.5 * values * (1.0 - tangent * tangent) * root_two_pi * (1.0 + 3.0 * cubic_coef * values * values)


def angles(left_idx, right_idx, length):
    product_idx = (left_idx[:, None] * right_idx[None, :]) % length
    return (2.0 * jnp.pi / length) * product_idx.astype(jnp.float32)


def tables(length, mode_count):
    cell_idx = jnp.arange(length, dtype=jnp.int32)
    low_modes = jnp.arange(mode_count, dtype=jnp.int32)
    both_modes = jnp.concatenate([low_modes, low_modes + (length - mode_count)])
    along_w = angles(cell_idx, low_modes, length)
    cos_w = jnp.cos(along_w)
    sin_w = jnp.sin(along_w)
    row_table = jnp.stack([cos_w, -sin_w], axis=1).astype(jnp.bfloat16)
    weight = jnp.where(low_modes == 0, 1.0, 2.0).astype(jnp.float32)[:, None]
    back_table = jnp.stack([weight * cos_w.T, -weight * sin_w.T], axis=1).astype(jnp.bfloat16)
    along_h = angles(cell_idx, both_modes, length)
    cos_h = jnp.cos(along_h)
    sin_h = jnp.sin(along_h)
    col_table = jnp.stack([jnp.stack([cos_h, -sin_h], axis=1), jnp.stack([sin_h, cos_h], axis=1)], axis=0).astype(jnp.bfloat16)
    return row_table, back_table, col_table


def product(form, left, right):
    return jnp.einsum(form, left.astype(jnp.float32), right.astype(jnp.float32), precision=lax.Precision.HIGHEST)


def mix_modes(spec_layer, mode_spec):
    real_weight = spec_layer[:, 0]
    imag_weight = spec_layer[:, 1]
    real_mode = mode_spec[:, :, 0]
    imag_mode = mode_spec[:, :, 1]
    out_real = product('koix,kix->kox', real_weight, real_mode) - product('koix,kix->kox', imag_weight, imag_mode)
    out_imag = product('koix,kix->kox', real_weight, imag_mode) + product('koix,kix->kox', imag_weight, real_mode)
    return jnp.stack([out_real, out_imag], axis=1)


def mix_adjoint(spec_layer, mode_spec, grad_mixed):
    real_weight = spec_layer[:, 0]
    imag_weight = spec_layer[:, 1]
    real_mode = mode_spec[:, :, 0]
    imag_mode = mode_spec[:, :, 1]
    real_grad = grad_mixed[:, 0]
    imag_grad = grad_mixed[:, 1]
    grad_real = product('koix,kox->kix', real_weight, real_grad) + product('koix,kox->kix', imag_weight, imag_grad)
    grad_imag = product('koix,kox->kix', real_weight, imag_grad) - product('koix,kox->kix', imag_weight, real_grad)
    spec_real = product('kox,kix->koix', real_grad, real_mode) + product('kox,kix->koix', imag_grad, imag_mode)
    spec_imag = product('kox,kix->koix', imag_grad, real_mode) - product('kox,kix->koix', real_grad, imag_mode)
    return jnp.stack([grad_real, grad_imag], axis=2), jnp.stack([spec_real, spec_imag], axis=1)


def layer_forward(activity, skip_layer, up_layer, down_layer, spec_layer, table_set):
    row_table, back_table, col_table = table_set
    length = activity.shape[2]
    row_spec = product('chw,wpk->kpch', activity, row_table).astype(jnp.bfloat16)
    mode_spec = (product('kpch,phqx->kcqx', row_spec, col_table) / length).astype(jnp.bfloat16)
    mixed_modes = mix_modes(spec_layer, mode_spec).astype(jnp.bfloat16)
    back_spec = product('kqcx,phqx->kpch', mixed_modes, col_table).astype(jnp.bfloat16)
    spectral = product('kpch,kpw->chw', back_spec, back_table) / length
    pre_act = spectral + product('oc,chw->ohw', skip_layer, activity)
    gated_act = smooth_gate(pre_act).astype(jnp.bfloat16)
    hidden = product('fc,chw->fhw', up_layer, gated_act)
    inner_act = smooth_gate(hidden).astype(jnp.bfloat16)
    result = (activity.astype(jnp.float32) + product('cf,fhw->chw', down_layer, inner_act)).astype(jnp.bfloat16)
    return result, (activity, mode_spec, pre_act, gated_act, hidden, inner_act)


def layer_backward(grad_out, saved_act, skip_layer, up_layer, down_layer, spec_layer, table_set):
    row_table, back_table, col_table = table_set
    activity, mode_spec, pre_act, gated_act, hidden, inner_act = saved_act
    length = activity.shape[2]
    grad_inner = product('cf,chw->fhw', down_layer, grad_out)
    grad_down = product('chw,fhw->cf', grad_out, inner_act) / length
    grad_hidden = (grad_inner * gate_slope(hidden)).astype(jnp.bfloat16)
    grad_gated = product('fc,fhw->chw', up_layer, grad_hidden)
    grad_up = product('fhw,chw->fc', grad_hidden, gated_act) / length
    grad_pre = (grad_gated * gate_slope(pre_act)).astype(jnp.bfloat16)
    grad_skip = product('ohw,chw->oc', grad_pre, activity) / length
    grad_back = (product('chw,kpw->kpch', grad_pre, back_table) / length).astype(jnp.bfloat16)
    grad_mixed = product('kpch,phqx->kqcx', grad_back, col_table).astype(jnp.bfloat16)
    grad_modes, grad_spec = mix_adjoint(spec_layer, mode_spec, grad_mixed)
    grad_rows = (product('kcqx,phqx->kpch', grad_modes.astype(jnp.bfloat16), col_table) / length).astype(jnp.bfloat16)
    grad_field = grad_out.astype(jnp.float32) + product('oc,ohw->chw', skip_layer, grad_pre) + product('kpch,wpk->chw', grad_rows, row_table)
    return grad_field.astype(jnp.bfloat16), grad_skip, grad_up, grad_down, grad_spec


def reference(emitted, returned, stash, skip_w, up_w, down_w, spec_w):
    length = emitted.shape[3]
    table_set = tables(length, M)
    ahead_all = jnp.roll(emitted, 1, axis=0)
    top_all = jnp.roll(returned, -1, axis=0)
    kept_all = jnp.roll(stash, SECTIONS // 2, axis=0)

    def section_work(inputs):
        ahead_input, top_grad, kept_input, skip_section, up_section, down_section, spec_section = inputs
        activity = ahead_input
        for layer_idx in range(LAYERS):
            activity, unused_keep = layer_forward(activity, skip_section[layer_idx], up_section[layer_idx], down_section[layer_idx], spec_section[layer_idx], table_set)
        sent_out = activity
        activity = kept_input
        saved_list = []
        for layer_idx in range(LAYERS):
            activity, layer_keep = layer_forward(activity, skip_section[layer_idx], up_section[layer_idx], down_section[layer_idx], spec_section[layer_idx], table_set)
            saved_list.append(layer_keep)
        grad_now = top_grad
        skip_list, up_list, down_list, spec_list = [], [], [], []
        for layer_idx in reversed(range(LAYERS)):
            grad_now, grad_skip, grad_up, grad_down, grad_spec = layer_backward(grad_now, saved_list[layer_idx], skip_section[layer_idx], up_section[layer_idx], down_section[layer_idx], spec_section[layer_idx], table_set)
            skip_list.insert(0, grad_skip)
            up_list.insert(0, grad_up)
            down_list.insert(0, grad_down)
            spec_list.insert(0, grad_spec)
        return sent_out, grad_now, jnp.stack(skip_list), jnp.stack(up_list), jnp.stack(down_list), jnp.stack(spec_list)

    sent, back_grad, grad_skip, grad_up, grad_down, grad_spec = lax.map(section_work, (ahead_all, top_all, kept_all, skip_w, up_w, down_w, spec_w))
    return (sent, back_grad, grad_skip, grad_up, grad_down, grad_spec)
```

```python
import functools

import jax
import jax.numpy as jnp
import numpy as np
import ml_dtypes
from jax import lax
from jax.experimental import pallas as pl
from jax.experimental.pallas import tpu as pltpu
from jax.sharding import PartitionSpec as P

M = 64
LAYERS = 2
N = 512
C = 20
F = 80
SLABS = 8
ROWS = N // SLABS
KB = M // SLABS
CP = C // 2
EARLY = CP // 2
WIRE = C * KB
LANES = 128
BF = jnp.bfloat16
F32 = jnp.float32

root_two_pi = 0.7978845608028654
cubic_coef = 0.044715


def np_angles(left_idx, right_idx, length):
    product_idx = left_idx[:, None] * right_idx[None, :] % length
    return np.float32(2.0 * np.pi / length) * product_idx.astype(np.float32)


def np_tables():
    cell = np.arange(N)
    low = np.arange(M)
    both = np.concatenate([low, low + (N - M)])
    along_w = np_angles(cell, low, N)
    cos_w, sin_w = np.cos(along_w), np.sin(along_w)
    row = np.stack([cos_w.T, -sin_w.T], 0)
    weight = np.where(low == 0, 1.0, 2.0).astype(np.float32)[None, :, None]
    back = row * weight
    along_h = np_angles(cell, both, N)
    cos_h, sin_h = np.cos(along_h), np.sin(along_h)
    col = np.stack([np.stack([cos_h, -sin_h], 1), np.stack([sin_h, cos_h], 1)], 0)
    col = col.reshape(2, SLABS, ROWS, 2, 2 * M).transpose(1, 0, 2, 3, 4).reshape(SLABS, 2 * ROWS, 4 * M)

    def forward(table, scale):
        t = table.reshape(2, SLABS, KB, N).transpose(1, 0, 2, 3).reshape(2 * M, N)
        return (t.astype(ml_dtypes.bfloat16).astype(np.float32) * scale).astype(ml_dtypes.bfloat16)

    def inverse(table, scale):
        t = table.reshape(2, SLABS, KB, N)
        out = np.zeros((2, 2, SLABS, 2, KB, N), np.float32)
        for c in range(2):
            out[c, :, :, c] = t
        out = out.reshape(2, 4 * M, N)
        return (out.astype(ml_dtypes.bfloat16).astype(np.float32) * scale).astype(ml_dtypes.bfloat16)

    return {
        "ew": forward(row, 1.0),
        "ei": forward(back, 1.0 / N),
        "ewz": inverse(row, 1.0),
        "eiz": inverse(back, 1.0 / N),
        "col": col.astype(ml_dtypes.bfloat16),
    }


def dot(a, b):
    return jnp.dot(a, b, preferred_element_type=F32)


def dot_nt(a, b):
    return lax.dot_general(a, b, (((1,), (1,)), ((), ())), preferred_element_type=F32)


def gate(t):
    t = t.astype(BF)
    u = t * (BF(root_two_pi) + BF(root_two_pi * cubic_coef) * (t * t))
    half = BF(0.5) * t
    return half + half * jnp.tanh(u)


def gate_and_slope(t):
    t = t.astype(BF)
    tt = t * t
    th = jnp.tanh(t * (BF(root_two_pi) + BF(root_two_pi * cubic_coef) * tt))
    half = BF(0.5) * t
    value = half + half * th
    slope = (BF(0.5) + BF(0.5) * th) + half * (BF(1.0) - th * th) * (
        BF(root_two_pi) + BF(3.0 * root_two_pi * cubic_coef) * tt
    )
    return value, slope


def rows_to_wire(read, table_ref, send_ref):
    lane = lax.broadcasted_iota(jnp.int32, (M, LANES), 1)
    low = lane < ROWS
    table = table_ref[...]
    for cp in range(0, CP, 2):
        res = dot_nt(table, read(cp, 2))
        for s in range(2):
            r = res[:, s * LANES : (s + 1) * LANES].reshape(SLABS, 2, KB, LANES)
            a = r[:, 0].reshape(M, LANES)
            b = r[:, 1].reshape(M, LANES)
            lo = jnp.where(low, a, pltpu.roll(b, ROWS, 1)).reshape(SLABS, 1, KB, LANES)
            hi = jnp.where(low, pltpu.roll(a, ROWS, 1), b).reshape(SLABS, 1, KB, LANES)
            out = jnp.concatenate([lo, hi], axis=1).reshape(SLABS, 2 * KB, LANES).astype(BF)
            at = (cp + s) * 2 * KB
            send_ref[:, at : at + 2 * KB, :] = out


def wire_to_rows(recv_ref, left_ref):
    for cp in range(CP):
        m = recv_ref[:, cp * 2 * KB : (cp + 1) * 2 * KB, :].reshape(2 * M, LANES)
        t = m.astype(F32).T.astype(BF)
        left_ref[cp * ROWS : (cp + 1) * ROWS, 0 : 2 * M] = t[:ROWS]
        left_ref[cp * ROWS : (cp + 1) * ROWS, 2 * M : 4 * M] = t[ROWS:]


def wide(block):
    x = block.astype(F32)
    return jnp.concatenate([x[:, :, s * 8 : s * 8 + 8, :].reshape(8 * C, N) for s in range(2)], axis=1)


def narrow(x):
    parts = [x[:, s * N : (s + 1) * N].reshape(CP, 2, 8, N) for s in range(2)]
    return jnp.concatenate(parts, axis=2).astype(BF)


def field_read(ref):
    def read(cp, pairs):
        return ref[cp : cp + pairs].reshape(pairs * 2 * ROWS, N)

    return read


def row_dft_body(v_ref, table_ref, *rest):
    send_ref = rest[-1]
    rows_to_wire(field_read(v_ref), table_ref, send_ref)


def forward_body(keep, last, *refs):
    u_ref, v_ref, ws_ref, w1_ref, w2_ref, eiz_ref, ew_ref = refs[:7]
    outs = list(refs[7:])
    left_ref, z_ref = outs[-2:]
    outs = outs[:-2]
    out_ref = outs[0]
    at = 1
    if not last:
        send_ref = outs[at]
        at += 1
    if keep:
        y_ref, slope_ref = outs[at : at + 2]
    wire_to_rows(u_ref, left_ref)
    for c2 in range(2):
        z_ref[:, c2] = dot(left_ref[...], eiz_ref[c2]).reshape(CP, ROWS, N)

    def step(i, carry):
        h0 = pl.multiple_of(i * 16, 16)
        where = (slice(None), slice(None), pl.ds(h0, 16))
        v = wide(v_ref[where])
        z = wide(z_ref[where]) + dot(ws_ref[...], v.astype(BF))
        if keep:
            y, slope = gate_and_slope(z)
            y_ref[where] = narrow(y.astype(F32))
            slope_ref[where] = narrow(slope.astype(F32))
        else:
            y = gate(z)
        hidden = dot(w1_ref[...], y.astype(BF))
        out_ref[where] = narrow(v + dot(w2_ref[...], gate(hidden)))
        return carry

    lax.fori_loop(0, ROWS // 16, step, 0)
    if not last:
        rows_to_wire(field_read(out_ref), ew_ref, send_ref)


def back_body(first, layer, *refs):
    refs = list(refs)
    u_ref, table_ref, v_ref, wst_ref, w1_ref, w1t_ref, w2t_ref, ei_ref = refs[:8]
    if first:
        g_ref, ws_ref = refs[8:10]
        refs = refs[10:]
    else:
        base_in_ref, grads_in_ref, y_ref, slope_ref = refs[8:12]
        refs = refs[12:]
    base_ref, send_ref, grads_ref, gz_ref, gd_ref, gu_ref, gs_ref, left_ref, field_ref = refs
    wire_to_rows(u_ref, left_ref)
    for c2 in range(2):
        r = dot(left_ref[...], table_ref[c2]).reshape(CP, ROWS, N)
        if not first:
            r = (base_in_ref[:, c2].astype(F32) + r).astype(BF)
        field_ref[:, c2] = r
    if not first:
        g_ref = field_ref
    gd_ref[...] = jnp.zeros_like(gd_ref)
    gu_ref[...] = jnp.zeros_like(gu_ref)
    gs_ref[...] = jnp.zeros_like(gs_ref)

    def step(i, carry):
        h0 = pl.multiple_of(i * 16, 16)
        where = (slice(None), slice(None), pl.ds(h0, 16))
        g = wide(g_ref[where])
        gb = g.astype(BF)
        v = wide(v_ref[where]).astype(BF)
        if first:
            y, out_slope = gate_and_slope(wide(field_ref[where]) + dot(ws_ref[...], v))
            out_slope = out_slope.astype(F32)
        else:
            y = wide(y_ref[where]).astype(BF)
            out_slope = wide(slope_ref[where])
        act, slope = gate_and_slope(dot(w1_ref[...], y))
        gh = dot(w2t_ref[...], gb).astype(BF) * slope
        gz = (dot(w1t_ref[...], gh) * out_slope).astype(BF)
        base_ref[where] = narrow(g + dot(wst_ref[...], gz))
        gz_ref[where] = narrow(gz.astype(F32))
        gd_ref[...] += dot_nt(act.astype(BF), gb)
        gu_ref[...] += dot_nt(gh, y)
        gs_ref[...] += dot_nt(gz, v)
        return carry

    lax.fori_loop(0, ROWS // 16, step, 0)
    rows_to_wire(field_read(gz_ref), ei_ref, send_ref)
    total = jnp.zeros((F, LANES), F32) if first else grads_in_ref[...]
    for ref, slot in ((gd_ref, 0), (gu_ref, 1), (gs_ref, 2)):
        rows, cols = ref.shape
        r_idx = lax.broadcasted_iota(jnp.int32, (rows, cols), 0) % 8
        c_idx = lax.broadcasted_iota(jnp.int32, (rows, cols), 1) % 8
        kept = jnp.where(r_idx == c_idx, ref[...], 0.0).reshape(rows // 8, 8, cols)
        summed = jnp.sum(kept, axis=1)
        offset = (slot * 2 + layer) * C
        pick_r = lax.broadcasted_iota(jnp.int32, (cols, LANES), 0) // 8 + offset
        pick_c = lax.broadcasted_iota(jnp.int32, (cols, LANES), 1)
        pick = jnp.where(pick_r == pick_c, 1.0 / N, 0.0).astype(F32)
        placed = jnp.dot(summed, pick, precision=lax.Precision.HIGHEST, preferred_element_type=F32)
        if rows // 8 < F:
            placed = jnp.concatenate([placed, jnp.zeros((F - rows // 8, LANES), F32)], axis=0)
        total = total + placed
    grads_ref[...] = total


def finish_body(recv_ref, base_ref, ewz_ref, out_ref, grads_ref, left_ref):
    wire_to_rows(recv_ref, left_ref)
    for c2 in range(2):
        r = dot(left_ref[...], ewz_ref[c2]).reshape(CP, ROWS, N)
        out_ref[:, c2] = (base_ref[:, c2].astype(F32) + r).astype(BF)
    grads_ref[...] = jnp.sum(recv_ref[:, WIRE : WIRE + F, :].astype(F32), axis=0)


def to_spectrum(recv_ref, col_ref):
    total = jnp.zeros((WIRE, 4 * M), F32)
    for j in range(SLABS):
        total = total + dot(recv_ref[j], col_ref[j])
    return total


def from_spectrum(values, col_ref, send_ref, scale):
    for j in range(SLABS):
        r = dot_nt(values, col_ref[j])
        if scale != 1.0:
            r = r * scale
        send_ref[j, 0:WIRE, :] = r.astype(BF)


def spectrum_in(ref, value):
    value = value.astype(F32)
    ref[0] = value[:, :LANES]
    ref[1] = value[:, LANES:]


def spectrum_of(ref):
    return jnp.concatenate([ref[0], ref[1]], axis=1).astype(BF)


def interleaved(xa_ref, xb_ref, value):
    value = value.astype(F32)
    re = value[:, :LANES].reshape(C, KB, LANES)
    im = value[:, LANES:].reshape(C, KB, LANES)
    for c in range(C):
        xa_ref[pl.ds(2 * c, KB, stride=2 * C), :] = re[c]
        xa_ref[pl.ds(2 * c + 1, KB, stride=2 * C), :] = -im[c]
        xb_ref[pl.ds(2 * c, KB, stride=2 * C), :] = im[c]
        xb_ref[pl.ds(2 * c + 1, KB, stride=2 * C), :] = re[c]


def mix(spec_ref, xa_ref, xb_ref, y_ref):
    def one(k, carry):
        at = pl.multiple_of(k * 2 * C, 8)
        xa = xa_ref[pl.ds(at, 2 * C), :]
        xb = xb_ref[pl.ds(at, 2 * C), :]
        for o in range(0, C, 2):
            w = spec_ref[k, o * 2 * C : (o + 2) * 2 * C, :].astype(F32)
            for s in range(2):
                r = w[s * 2 * C : (s + 1) * 2 * C]
                row = pl.ds((o + s) * KB + k, 1)
                y_ref[0, row, :] = jnp.sum(r * xa, axis=0, keepdims=True)
                y_ref[1, row, :] = jnp.sum(r * xb, axis=0, keepdims=True)
        return carry

    lax.fori_loop(0, KB, one, 0)


def spectrum_body(recv_ref, col_ref, x_ref):
    x_ref[...] = (to_spectrum(recv_ref, col_ref) * (1.0 / N)).astype(BF)


def mix_body(x_ref, spec_ref, col_ref, *rest):
    send_ref, xa_ref, xb_ref, ys_ref = rest[-4:]
    interleaved(xa_ref, xb_ref, x_ref[...])
    mix(spec_ref, xa_ref, xb_ref, ys_ref)
    from_spectrum(spectrum_of(ys_ref), col_ref, send_ref, 1.0)


def modes_body(recv_ref, spec_ref, col_ref, *rest):
    x_ref, send_ref, xa_ref, xb_ref, ys_ref = rest[-5:]
    x = (to_spectrum(recv_ref, col_ref) * (1.0 / N)).astype(BF)
    x_ref[...] = x
    interleaved(xa_ref, xb_ref, x)
    mix(spec_ref, xa_ref, xb_ref, ys_ref)
    from_spectrum(spectrum_of(ys_ref), col_ref, send_ref, 1.0)


def modes_back_body(tail, *refs):
    refs = list(refs)
    recv_ref, spec_ref, col_ref = refs[:3]
    refs = refs[3:]
    if tail:
        grads_ref = refs.pop(0)
    send_ref, gy_ref, ga_ref, gb_ref, ys_ref, gx_ref = refs
    gy = to_spectrum(recv_ref, col_ref).astype(BF)
    gy_ref[...] = gy
    spectrum_in(ys_ref, gy)

    def one(k, carry):
        acc_a = jnp.zeros((2 * C, LANES), F32)
        acc_b = jnp.zeros((2 * C, LANES), F32)
        for o in range(0, C, 2):
            w = spec_ref[k, o * 2 * C : (o + 2) * 2 * C, :].astype(F32)
            for s in range(2):
                r = w[s * 2 * C : (s + 1) * 2 * C]
                row = pl.ds((o + s) * KB + k, 1)
                acc_a = acc_a + r * ys_ref[0, row, :]
                acc_b = acc_b + r * ys_ref[1, row, :]
        at = pl.multiple_of(k * 2 * C, 8)
        ga_ref[pl.ds(at, 2 * C), :] = acc_a
        gb_ref[pl.ds(at, 2 * C), :] = acc_b
        return carry

    lax.fori_loop(0, KB, one, 0)
    for c in range(C):
        re = pl.ds(2 * c, KB, stride=2 * C)
        im = pl.ds(2 * c + 1, KB, stride=2 * C)
        gx_ref[0, c * KB : (c + 1) * KB, :] = ga_ref[re, :] + gb_ref[im, :]
        gx_ref[1, c * KB : (c + 1) * KB, :] = gb_ref[re, :] - ga_ref[im, :]
    from_spectrum(spectrum_of(gx_ref), col_ref, send_ref, 1.0 / N)
    if tail:
        g = grads_ref[...].astype(BF)
        for j in range(SLABS):
            send_ref[j, WIRE : WIRE + F, :] = g


def spec_grad_body(gy_ref, x_ref, *rest):
    out_ref, ys_ref, xa_ref, xb_ref = rest[-4:]
    k = pl.program_id(0)

    @pl.when(k == 0)
    def _():
        spectrum_in(ys_ref, gy_ref[...])
        interleaved(xa_ref, xb_ref, x_ref[...])

    at = pl.multiple_of(k * 2 * C, 8)
    xa = xa_ref[pl.ds(at, 2 * C), :]
    xb = xb_ref[pl.ds(at, 2 * C), :]
    for o in range(C):
        row = pl.ds(o * KB + k, 1)
        out_ref[o * 2 * C : (o + 1) * 2 * C, :] = ys_ref[0, row, :] * xa + ys_ref[1, row, :] * xb


def prep_body(skip_ref, up_ref, down_ref, ws_ref, wst_ref, w1_ref, w1t_ref, w2_ref, w2t_ref):
    def spread(rows):
        r = lax.broadcasted_iota(jnp.int32, (8 * rows, rows), 0) // 8
        c = lax.broadcasted_iota(jnp.int32, (8 * rows, rows), 1)
        return jnp.where(r == c, 1.0, 0.0).astype(BF)

    wide = {n: spread(n) for n in (C, F)}

    def same(rows, cols):
        r = lax.broadcasted_iota(jnp.int32, (8 * rows, 8 * cols), 0) % 8
        c = lax.broadcasted_iota(jnp.int32, (8 * rows, 8 * cols), 1) % 8
        return r == c

    masks = {(a, b): same(a, b) for a, b in ((C, C), (F, C), (C, F))}

    def expand(weight, a, b, straight_ref, turned_ref, layer):
        rows = dot(wide[a], weight).astype(BF)
        full = dot_nt(rows, wide[b])
        straight_ref[layer] = jnp.where(masks[a, b], full, 0.0).astype(BF)
        cols = dot_nt(wide[b], weight).astype(BF)
        full = dot_nt(cols, wide[a])
        turned_ref[layer] = jnp.where(masks[b, a], full, 0.0).astype(BF)

    for layer in range(LAYERS):
        expand(skip_ref[layer], C, C, ws_ref, wst_ref, layer)
        expand(up_ref[layer], F, C, w1_ref, w1t_ref, layer)
        expand(down_ref[layer], C, F, w2_ref, w2t_ref, layer)


FIELD = (CP, 2, ROWS, N)
LIMIT = pltpu.CompilerParams(vmem_limit_bytes=60 * 1024 * 1024)


def full(shape):
    zeros = (0,) * len(shape)
    return pl.BlockSpec(tuple(shape), lambda *_: zeros)


def part(shape, index):
    return pl.BlockSpec(tuple(shape), lambda *_: tuple(index))


def wire_part(slot, rows=WIRE):
    return part((SLABS, rows, LANES), (0, slot, 0))


def layer_part(shape, layer):
    return part((None,) + tuple(shape), (layer,) + (0,) * len(shape))


def spec_part(layer):
    return part((None, KB, 2 * C * C, LANES), (layer, 0, 0, 0))


def shape_of(shape, dtype):
    return jax.ShapeDtypeStruct(tuple(shape), dtype)


def call(body, name, args, outs, scratch=(), into=None):
    arrays = [a for a, _ in args]
    specs = [s for _, s in args]
    aliases = {}
    if into is not None:
        aliases = {len(arrays): into[0]}
        arrays.append(into[1])
        specs.append(pl.BlockSpec(memory_space=pl.ANY))
        inner, count = body, len(arrays)

        def body(*refs):
            inner(*refs[: count - 1], *refs[count:])

    return pl.pallas_call(
        body,
        out_shape=[o for o, _ in outs],
        grid_spec=pltpu.PrefetchScalarGridSpec(
            num_scalar_prefetch=0,
            grid=(1,),
            in_specs=specs,
            out_specs=[s for _, s in outs],
            scratch_shapes=list(scratch),
        ),
        input_output_aliases=aliases,
        compiler_params=LIMIT,
        name=name,
    )(*arrays)


FIELD_OUT = (shape_of(FIELD, BF), full(FIELD))
LEFT = pltpu.VMEM((CP * ROWS, 4 * M), BF)


def row_dft(field, tabs, slot, slots, into=None):
    out = (shape_of((SLABS, slots * WIRE, LANES), BF), wire_part(slot))
    return call(
        row_dft_body,
        "row_dft",
        [(field, full(FIELD)), (tabs["ew"], full((2 * M, N)))],
        [out],
        into=None if into is None else (0, into),
    )[0]


def forward_rows(wire, slot, field, kron, layer, tabs, keep, last, send_slot=0, slots=1, into=None):
    outs = [FIELD_OUT]
    if not last:
        outs.append((shape_of((SLABS, slots * WIRE, LANES), BF), wire_part(send_slot)))
    if keep:
        outs += [FIELD_OUT, FIELD_OUT]
    return call(
        functools.partial(forward_body, keep, last),
        "forward_rows",
        [
            (wire, wire_part(slot)),
            (field, full(FIELD)),
            (kron["ws"], layer_part((8 * C, 8 * C), layer)),
            (kron["w1"], layer_part((8 * F, 8 * C), layer)),
            (kron["w2"], layer_part((8 * C, 8 * F), layer)),
            (tabs["eiz"], full((2, 4 * M, N))),
            (tabs["ew"], full((2 * M, N))),
        ],
        outs,
        scratch=[LEFT, pltpu.VMEM(FIELD, F32)],
        into=None if into is None else (1, into),
    )


def back_rows(first, layer, wire, field, kron, tabs, top=None, base=None, grads=None, y=None, slope=None):
    args = [
        (wire, wire_part(0)),
        (tabs["eiz" if first else "ewz"], full((2, 4 * M, N))),
        (field, full(FIELD)),
        (kron["wst"], layer_part((8 * C, 8 * C), layer)),
        (kron["w1"], layer_part((8 * F, 8 * C), layer)),
        (kron["w1t"], layer_part((8 * C, 8 * F), layer)),
        (kron["w2t"], layer_part((8 * F, 8 * C), layer)),
        (tabs["ei"], full((2 * M, N))),
    ]
    if first:
        args += [(top, full(FIELD)), (kron["ws"], layer_part((8 * C, 8 * C), layer))]
    else:
        args += [(base, full(FIELD)), (grads, full((F, LANES))), (y, full(FIELD)), (slope, full(FIELD))]
    scratch = [
        pltpu.VMEM(FIELD, BF),
        pltpu.VMEM((8 * F, 8 * C), F32),
        pltpu.VMEM((8 * F, 8 * C), F32),
        pltpu.VMEM((8 * C, 8 * C), F32),
        LEFT,
        pltpu.VMEM(FIELD, F32 if first else BF),
    ]
    return call(
        functools.partial(back_body, first, layer),
        "back_rows",
        args,
        [
            FIELD_OUT,
            (shape_of((SLABS, WIRE, LANES), BF), wire_part(0)),
            (shape_of((F, LANES), F32), full((F, LANES))),
        ],
        scratch=scratch,
    )


SPECTRUM = (WIRE, 4 * M)
SPECTRUM_OUT = (shape_of(SPECTRUM, BF), full(SPECTRUM))
HALF = pltpu.VMEM((2, WIRE, LANES), F32)
MIXED = pltpu.VMEM((2 * WIRE, LANES), F32)
COL = (SLABS, 2 * ROWS, 4 * M)


def spectrum(wire, slot, tabs):
    return call(
        spectrum_body, "spectrum", [(wire, wire_part(slot)), (tabs["col"], full(COL))], [SPECTRUM_OUT]
    )[0]


def mix_out(x, spec, layer, tabs, slot, slots, into=None):
    return call(
        mix_body,
        "mix_out",
        [(x, full(SPECTRUM)), (spec, spec_part(layer)), (tabs["col"], full(COL))],
        [(shape_of((SLABS, slots * WIRE, LANES), BF), wire_part(slot))],
        scratch=[MIXED, MIXED, HALF],
        into=None if into is None else (0, into),
    )[0]


def modes(wire, slot, spec, layer, tabs, send_slot, slots, into=None):
    return call(
        modes_body,
        "modes",
        [(wire, wire_part(slot)), (spec, spec_part(layer)), (tabs["col"], full(COL))],
        [SPECTRUM_OUT, (shape_of((SLABS, slots * WIRE, LANES), BF), wire_part(send_slot))],
        scratch=[MIXED, MIXED, HALF],
        into=None if into is None else (1, into),
    )


def modes_back(wire, spec, layer, tabs, grads=None, slots=1):
    tail = grads is not None
    rows = WIRE + (F if tail else 0)
    args = [(wire, wire_part(0)), (spec, spec_part(layer)), (tabs["col"], full(COL))]
    if tail:
        args.append((grads, full((F, LANES))))
    return call(
        functools.partial(modes_back_body, tail),
        "modes_back",
        args,
        [(shape_of((SLABS, slots * rows, LANES), BF), wire_part(0, rows)), SPECTRUM_OUT],
        scratch=[MIXED, MIXED, HALF, HALF],
    )


def spec_grad(gy, x, layer, into=None):
    args, specs, aliases = [gy, x], [full(SPECTRUM), full(SPECTRUM)], {}
    body = spec_grad_body
    if into is not None:
        args.append(into)
        specs.append(pl.BlockSpec(memory_space=pl.ANY))
        aliases = {2: 0}
    return pl.pallas_call(
        body,
        out_shape=shape_of((LAYERS, KB, 2 * C * C, LANES), F32),
        grid_spec=pltpu.PrefetchScalarGridSpec(
            num_scalar_prefetch=0,
            grid=(KB,),
            in_specs=specs,
            out_specs=pl.BlockSpec(
                (None, None, 2 * C * C, LANES), lambda k: (layer, k, 0, 0)
            ),
            scratch_shapes=[HALF, MIXED, MIXED],
        ),
        input_output_aliases=aliases,
        compiler_params=LIMIT,
        name="spec_grad",
    )(*args)


def finish(wire, base, tabs):
    rows = WIRE + F
    return call(
        finish_body,
        "finish",
        [(wire, wire_part(0, rows)), (base, full(FIELD)), (tabs["ewz"], full((2, 4 * M, N)))],
        [FIELD_OUT, (shape_of((F, LANES), F32), full((F, LANES)))],
        scratch=[LEFT],
    )


def prep(skip_w, up_w, down_w):
    names = ["ws", "wst", "w1", "w1t", "w2", "w2t"]
    sizes = [(C, C), (C, C), (F, C), (C, F), (C, F), (F, C)]
    outs = [(LAYERS, 8 * a, 8 * b) for a, b in sizes]
    res = call(
        prep_body,
        "prep",
        [(w, part((None,) + w.shape[1:], (0,) * w.ndim)) for w in (skip_w, up_w, down_w)],
        [(shape_of(o, BF), full(o)) for o in outs],
    )
    return dict(zip(names, res))


def exchange(wire):
    return lax.all_to_all(wire, "slab", split_axis=0, concat_axis=0, tiled=True)


def shifted(block, distance):
    count = lax.axis_size("section")
    return lax.ppermute(block, "section", [(i, (i + distance) % count) for i in range(count)])


def shards(emitted, returned, stash, skip_w, up_w, down_w, spec_w):
    tabs = {name: jnp.asarray(value) for name, value in np_tables().items()}
    half = lax.axis_size("section") // 2
    emitted = emitted.reshape(FIELD)
    returned = returned.reshape(FIELD)
    stash = stash.reshape(FIELD)
    spec_w = spec_w[0].transpose(0, 1, 3, 4, 2, 5).reshape(LAYERS, KB, 2 * C * C, LANES)
    kron = prep(skip_w, up_w, down_w)
    kept_a = shifted(stash[:EARLY], half)

    wire = row_dft(stash, tabs, 0, 2)
    wire = row_dft(emitted, tabs, 1, 2, into=wire)
    wire = exchange(wire)
    x_0 = shifted(spectrum(wire, 0, tabs), half)
    ahead_x = shifted(spectrum(wire, 1, tabs), 1)
    stash_b, emitted, x_0, ahead_x = lax.optimization_barrier((stash[EARLY:], emitted, x_0, ahead_x))
    kept_b = shifted(stash_b, half)
    ahead = shifted(emitted, 1)
    kept = jnp.concatenate([kept_a, kept_b], axis=0)

    wire = mix_out(x_0, spec_w, 0, tabs, 0, 2)
    wire = mix_out(ahead_x, spec_w, 0, tabs, 1, 2, into=wire)
    first_wire = exchange(wire)
    kept_1, out, y_0, slope_0 = forward_rows(first_wire, 0, kept, kron, 0, tabs, True, False)
    returned, out = lax.optimization_barrier((returned, out))
    wire = exchange(out)
    top = shifted(returned, -1)
    x_1, out = modes(wire, 0, spec_w, 1, tabs, 0, 2)
    ahead_1, out = forward_rows(first_wire, 1, ahead, kron, 0, tabs, False, False, 1, 2, into=out)
    second_wire = exchange(out)

    base, out, grads = back_rows(True, 1, second_wire, kept_1, kron, tabs, top=top)
    wire = exchange(out)
    out, gy_1 = modes_back(wire, spec_w, 1, tabs, slots=2)
    _, out = modes(second_wire, 1, spec_w, 1, tabs, 1, 2, into=out)
    third_wire = exchange(out)
    grad_spec = spec_grad(gy_1, x_1, 1)
    base, out, grads = back_rows(
        False, 0, third_wire, kept, kron, tabs, base=base, grads=grads, y=y_0, slope=slope_0
    )
    wire = exchange(out)
    (sent,) = forward_rows(third_wire, 1, ahead_1, kron, 1, tabs, False, True)
    out, gy_0 = modes_back(wire, spec_w, 0, tabs, grads)
    wire = exchange(out)
    grad_spec = spec_grad(gy_0, x_0, 0, into=grad_spec)
    back_grad, packed = finish(wire, base, tabs)

    def slot(number):
        return jnp.stack([packed[:, (number * 2 + l) * C : (number * 2 + l + 1) * C] for l in range(LAYERS)])

    grad_down = jnp.swapaxes(slot(0), 1, 2)
    grad_up = slot(1)
    grad_skip = slot(2)[:, :C]
    field = (1, C, ROWS, N)
    return (
        sent.reshape(field),
        back_grad.reshape(field),
        grad_skip[None],
        grad_up[None],
        grad_down[None],
        grad_spec.reshape(LAYERS, KB, C, C, 2, LANES).transpose(0, 1, 4, 2, 3, 5)[None],
    )


def solution(mesh):
    field = P("section", None, "slab", None)
    weight = P("section", None, None, None)
    spec = P("section", None, "slab", None, None, None, None)
    return jax.shard_map(
        shards,
        mesh=mesh,
        in_specs=(field, field, field, weight, weight, weight, spec),
        out_specs=(field, field, weight, weight, weight, spec),
        check_vma=False,
    )
```

```python
import functools

import jax
import jax.numpy as jnp
import numpy as np
import ml_dtypes
from jax import lax
from jax.experimental import pallas as pl
from jax.experimental.pallas import tpu as pltpu
from jax.sharding import PartitionSpec as P

M = 64
LAYERS = 2
N = 512
C = 20
F = 80
SLABS = 8
ROWS = N // SLABS
KB = M // SLABS
CP = C // 2
STEP = 4
CUTS = (CP // 2, CP * 4 // 5)
WIRE = C * KB
LANES = 128
BF = jnp.bfloat16
F32 = jnp.float32

root_two_pi = 0.7978845608028654
cubic_coef = 0.044715


def np_angles(left_idx, right_idx, length):
    product_idx = left_idx[:, None] * right_idx[None, :] % length
    return np.float32(2.0 * np.pi / length) * product_idx.astype(np.float32)


def np_tables():
    cell = np.arange(N)
    low = np.arange(M)
    both = np.concatenate([low, low + (N - M)])
    along_w = np_angles(cell, low, N)
    cos_w, sin_w = np.cos(along_w), np.sin(along_w)
    row = np.stack([cos_w.T, -sin_w.T], 0)
    weight = np.where(low == 0, 1.0, 2.0).astype(np.float32)[None, :, None]
    back = row * weight
    along_h = np_angles(cell, both, N)
    cos_h, sin_h = np.cos(along_h), np.sin(along_h)
    col = np.stack([np.stack([cos_h, -sin_h], 1), np.stack([sin_h, cos_h], 1)], 0)
    col = col.reshape(2, SLABS, ROWS, 2, 2 * M).transpose(1, 0, 2, 3, 4).reshape(SLABS, 2 * ROWS, 4 * M)

    def forward(table, scale):
        t = table.reshape(2, SLABS, KB, N).transpose(1, 0, 2, 3).reshape(2 * M, N)
        return (t.astype(ml_dtypes.bfloat16).astype(np.float32) * scale).astype(ml_dtypes.bfloat16)

    def inverse(table, scale):
        t = table.reshape(2, SLABS, KB, N)
        out = np.zeros((2, 2, SLABS, 2, KB, N), np.float32)
        for c in range(2):
            out[c, :, :, c] = t
        out = out.reshape(2, 4 * M, N)
        return (out.astype(ml_dtypes.bfloat16).astype(np.float32) * scale).astype(ml_dtypes.bfloat16)

    return {
        "ew": forward(row, 1.0),
        "ei": forward(back, 1.0 / N),
        "ewz": inverse(row, 1.0),
        "eiz": inverse(back, 1.0 / N),
        "col": col.astype(ml_dtypes.bfloat16),
    }


def dot(a, b):
    return jnp.dot(a, b, preferred_element_type=F32)


def dot_nt(a, b):
    return lax.dot_general(a, b, (((1,), (1,)), ((), ())), preferred_element_type=F32)


def gate(t):
    t = t.astype(BF)
    u = t * (BF(root_two_pi) + BF(root_two_pi * cubic_coef) * (t * t))
    half = BF(0.5) * t
    return half + half * jnp.tanh(u)


def gate_and_slope(t):
    t = t.astype(BF)
    tt = t * t
    th = jnp.tanh(t * (BF(root_two_pi) + BF(root_two_pi * cubic_coef) * tt))
    half = BF(0.5) * t
    value = half + half * th
    slope = (BF(0.5) + BF(0.5) * th) + half * (BF(1.0) - th * th) * (
        BF(root_two_pi) + BF(3.0 * root_two_pi * cubic_coef) * tt
    )
    return value, slope


def rows_to_wire(read, table_ref, send_ref):
    lane = lax.broadcasted_iota(jnp.int32, (M, LANES), 1)
    low = lane < ROWS
    table = table_ref[...]
    for cp in range(0, CP, 2):
        res = dot_nt(table, read(cp, 2))
        for s in range(2):
            r = res[:, s * LANES : (s + 1) * LANES].reshape(SLABS, 2, KB, LANES)
            a = r[:, 0].reshape(M, LANES)
            b = r[:, 1].reshape(M, LANES)
            lo = jnp.where(low, a, pltpu.roll(b, ROWS, 1)).reshape(SLABS, 1, KB, LANES)
            hi = jnp.where(low, pltpu.roll(a, ROWS, 1), b).reshape(SLABS, 1, KB, LANES)
            out = jnp.concatenate([lo, hi], axis=1).reshape(SLABS, 2 * KB, LANES).astype(BF)
            at = (cp + s) * 2 * KB
            send_ref[:, at : at + 2 * KB, :] = out


def wire_to_rows(recv_ref, left_ref):
    for cp in range(CP):
        m = recv_ref[:, cp * 2 * KB : (cp + 1) * 2 * KB, :].reshape(2 * M, LANES)
        t = m.astype(F32).T.astype(BF)
        left_ref[cp * ROWS : (cp + 1) * ROWS, 0 : 2 * M] = t[:ROWS]
        left_ref[cp * ROWS : (cp + 1) * ROWS, 2 * M : 4 * M] = t[ROWS:]


def wide(block):
    x = block.astype(F32)
    return jnp.concatenate([x[:, :, s * 8 : s * 8 + 8, :].reshape(8 * C, N) for s in range(2)], axis=1)


def both(refs, where):
    blocks = [ref[where] for ref in refs]
    return blocks[0] if len(blocks) == 1 else jnp.concatenate(blocks, axis=0)


def narrow(x):
    parts = [x[:, s * N : (s + 1) * N].reshape(CP, 2, 8, N) for s in range(2)]
    return jnp.concatenate(parts, axis=2).astype(BF)


def field_read(ref):
    def read(cp, pairs):
        return ref[cp : cp + pairs].reshape(pairs * 2 * ROWS, N)

    return read


def row_dft_body(v_ref, table_ref, *rest):
    send_ref = rest[-1]
    rows_to_wire(field_read(v_ref), table_ref, send_ref)


def forward_body(keep, last, parts, *refs):
    v_refs, refs = refs[:parts], refs[parts:]
    u_ref, ws_ref, w1_ref, w2_ref, eiz_ref, ew_ref = refs[:6]
    outs = list(refs[6:])
    left_ref, z_ref = outs[-2:]
    outs = outs[:-2]
    out_ref = outs[0]
    at = 1
    if not last:
        send_ref = outs[at]
        at += 1
    if keep:
        y_ref, slope_ref = outs[at : at + 2]
    wire_to_rows(u_ref, left_ref)
    for c2 in range(2):
        z_ref[:, c2] = dot(left_ref[...], eiz_ref[c2]).reshape(CP, ROWS, N)

    def step(i, carry):
        h0 = pl.multiple_of(i * 16, 16)
        where = (slice(None), slice(None), pl.ds(h0, 16))
        v = wide(both(v_refs, where))
        z = wide(z_ref[where]) + dot(ws_ref[...], v.astype(BF))
        if keep:
            y, slope = gate_and_slope(z)
            y_ref[where] = narrow(y.astype(F32))
            slope_ref[where] = narrow(slope.astype(F32))
        else:
            y = gate(z)
        hidden = dot(w1_ref[...], y.astype(BF))
        out_ref[where] = narrow(v + dot(w2_ref[...], gate(hidden)))
        return carry

    lax.fori_loop(0, ROWS // 16, step, 0)
    if not last:
        rows_to_wire(field_read(out_ref), ew_ref, send_ref)


def back_body(first, layer, parts, *refs):
    v_refs, refs = refs[:parts], refs[parts:]
    u_ref, table_ref, wst_ref, w1_ref, w1t_ref, w2t_ref, ei_ref = refs[:7]
    if first:
        g_ref, ws_ref = refs[7:9]
        refs = refs[9:]
    else:
        base_in_ref, grads_in_ref, y_ref, slope_ref = refs[7:11]
        refs = refs[11:]
    base_ref, send_ref, grads_ref, gz_ref, gd_ref, gu_ref, gs_ref, left_ref, field_ref = refs
    wire_to_rows(u_ref, left_ref)
    for c2 in range(2):
        r = dot(left_ref[...], table_ref[c2]).reshape(CP, ROWS, N)
        if not first:
            r = (base_in_ref[:, c2].astype(F32) + r).astype(BF)
        field_ref[:, c2] = r
    if not first:
        g_ref = field_ref
    gd_ref[...] = jnp.zeros_like(gd_ref)
    gu_ref[...] = jnp.zeros_like(gu_ref)
    gs_ref[...] = jnp.zeros_like(gs_ref)

    def step(i, carry):
        h0 = pl.multiple_of(i * 16, 16)
        where = (slice(None), slice(None), pl.ds(h0, 16))
        g = wide(g_ref[where])
        gb = g.astype(BF)
        v = wide(both(v_refs, where)).astype(BF)
        if first:
            y, out_slope = gate_and_slope(wide(field_ref[where]) + dot(ws_ref[...], v))
            out_slope = out_slope.astype(F32)
        else:
            y = wide(y_ref[where]).astype(BF)
            out_slope = wide(slope_ref[where])
        act, slope = gate_and_slope(dot(w1_ref[...], y))
        gh = dot(w2t_ref[...], gb).astype(BF) * slope
        gz = (dot(w1t_ref[...], gh) * out_slope).astype(BF)
        base_ref[where] = narrow(g + dot(wst_ref[...], gz))
        gz_ref[where] = narrow(gz.astype(F32))
        gd_ref[...] += dot_nt(act.astype(BF), gb)
        gu_ref[...] += dot_nt(gh, y)
        gs_ref[...] += dot_nt(v, gz)
        return carry

    lax.fori_loop(0, ROWS // 16, step, 0)
    rows_to_wire(field_read(gz_ref), ei_ref, send_ref)
    total = jnp.zeros((F, LANES), F32) if first else grads_in_ref[...]
    for ref, slot in ((gd_ref, 0), (gu_ref, 1), (gs_ref, 2)):
        rows, cols = ref.shape
        r_idx = lax.broadcasted_iota(jnp.int32, (rows, cols), 0) % 8
        c_idx = lax.broadcasted_iota(jnp.int32, (rows, cols), 1) % 8
        kept = jnp.where(r_idx == c_idx, ref[...], 0.0).reshape(rows // 8, 8, cols)
        summed = jnp.sum(kept, axis=1)
        offset = slot * 2 * C + layer
        pick_r = lax.broadcasted_iota(jnp.int32, (cols, LANES), 0) // 8 * 2 + offset
        pick_c = lax.broadcasted_iota(jnp.int32, (cols, LANES), 1)
        pick = jnp.where(pick_r == pick_c, 1.0 / N, 0.0).astype(F32)
        placed = jnp.dot(summed, pick, precision=lax.Precision.HIGHEST, preferred_element_type=F32)
        if rows // 8 < F:
            placed = jnp.concatenate([placed, jnp.zeros((F - rows // 8, LANES), F32)], axis=0)
        total = total + placed
    grads_ref[...] = total


def finish_body(recv_ref, base_ref, ewz_ref, out_ref, down_ref, up_ref, skip_ref, left_ref):
    wire_to_rows(recv_ref, left_ref)
    for c2 in range(2):
        r = dot(left_ref[...], ewz_ref[c2]).reshape(CP, ROWS, N)
        out_ref[:, c2] = (base_ref[:, c2].astype(F32) + r).astype(BF)
    grads = jnp.sum(recv_ref[:, WIRE : WIRE + F, :].astype(F32), axis=0).T
    down_ref[...] = grads[: 2 * C]
    up_ref[...] = grads[2 * C : 4 * C]
    skip_ref[...] = grads[4 * C : 6 * C, :C]


def to_spectrum(recv_ref, col_ref):
    total = jnp.zeros((WIRE, 4 * M), F32)
    for j in range(SLABS):
        total = total + dot(recv_ref[j], col_ref[j])
    return total


def from_spectrum(values, col_ref, send_ref, scale):
    for j in range(SLABS):
        r = dot_nt(values, col_ref[j])
        if scale != 1.0:
            r = r * scale
        send_ref[j, 0:WIRE, :] = r.astype(BF)


def spectrum_in(ref, value):
    value = value.astype(F32)
    ref[0] = value[:, :LANES]
    ref[1] = value[:, LANES:]


def spectrum_of(ref):
    return jnp.concatenate([ref[0], ref[1]], axis=1).astype(BF)


def interleaved(xa_ref, xb_ref, value):
    value = value.astype(F32)
    re = value[:, :LANES].reshape(C, KB, LANES)
    im = value[:, LANES:].reshape(C, KB, LANES)
    for c in range(C):
        xa_ref[pl.ds(2 * c, KB, stride=2 * C), :] = re[c]
        xa_ref[pl.ds(2 * c + 1, KB, stride=2 * C), :] = -im[c]
        xb_ref[pl.ds(2 * c, KB, stride=2 * C), :] = im[c]
        xb_ref[pl.ds(2 * c + 1, KB, stride=2 * C), :] = re[c]


def mix(spec_ref, xa_ref, xb_ref, y_ref):
    def one(k, carry):
        at = pl.multiple_of(k * 2 * C, 8)
        xa = xa_ref[pl.ds(at, 2 * C), :]
        xb = xb_ref[pl.ds(at, 2 * C), :]
        for o in range(0, C, 2):
            w = spec_ref[k, o * 2 * C : (o + 2) * 2 * C, :].astype(F32)
            for s in range(2):
                r = w[s * 2 * C : (s + 1) * 2 * C]
                row = pl.ds((o + s) * KB + k, 1)
                y_ref[0, row, :] = jnp.sum(r * xa, axis=0, keepdims=True)
                y_ref[1, row, :] = jnp.sum(r * xb, axis=0, keepdims=True)
        return carry

    lax.fori_loop(0, KB, one, 0)


def spectrum_body(recv_ref, col_ref, x_ref):
    x_ref[...] = (to_spectrum(recv_ref, col_ref) * (1.0 / N)).astype(BF)


def mix_body(x_ref, spec_ref, col_ref, *rest):
    send_ref, xa_ref, xb_ref, ys_ref = rest[-4:]
    interleaved(xa_ref, xb_ref, x_ref[...])
    mix(spec_ref, xa_ref, xb_ref, ys_ref)
    from_spectrum(spectrum_of(ys_ref), col_ref, send_ref, 1.0)


def modes_body(recv_ref, spec_ref, col_ref, *rest):
    x_ref, send_ref, xa_ref, xb_ref, ys_ref = rest[-5:]
    x = (to_spectrum(recv_ref, col_ref) * (1.0 / N)).astype(BF)
    x_ref[...] = x
    interleaved(xa_ref, xb_ref, x)
    mix(spec_ref, xa_ref, xb_ref, ys_ref)
    from_spectrum(spectrum_of(ys_ref), col_ref, send_ref, 1.0)


def modes_back_body(tail, *refs):
    refs = list(refs)
    recv_ref, spec_ref, col_ref = refs[:3]
    refs = refs[3:]
    if tail:
        grads_ref = refs.pop(0)
    send_ref, gy_ref, ga_ref, gb_ref, ys_ref, gx_ref = refs
    gy = to_spectrum(recv_ref, col_ref).astype(BF)
    gy_ref[...] = gy
    spectrum_in(ys_ref, gy)

    def one(k, carry):
        acc_a = jnp.zeros((2 * C, LANES), F32)
        acc_b = jnp.zeros((2 * C, LANES), F32)
        for o in range(0, C, 2):
            w = spec_ref[k, o * 2 * C : (o + 2) * 2 * C, :].astype(F32)
            for s in range(2):
                r = w[s * 2 * C : (s + 1) * 2 * C]
                row = pl.ds((o + s) * KB + k, 1)
                acc_a = acc_a + r * ys_ref[0, row, :]
                acc_b = acc_b + r * ys_ref[1, row, :]
        at = pl.multiple_of(k * 2 * C, 8)
        ga_ref[pl.ds(at, 2 * C), :] = acc_a
        gb_ref[pl.ds(at, 2 * C), :] = acc_b
        return carry

    lax.fori_loop(0, KB, one, 0)
    for c in range(C):
        re = pl.ds(2 * c, KB, stride=2 * C)
        im = pl.ds(2 * c + 1, KB, stride=2 * C)
        gx_ref[0, c * KB : (c + 1) * KB, :] = ga_ref[re, :] + gb_ref[im, :]
        gx_ref[1, c * KB : (c + 1) * KB, :] = gb_ref[re, :] - ga_ref[im, :]
    from_spectrum(spectrum_of(gx_ref), col_ref, send_ref, 1.0 / N)
    if tail:
        g = grads_ref[...].astype(BF)
        for j in range(SLABS):
            send_ref[j, WIRE : WIRE + F, :] = g


def spec_grad_body(gy_ref, x_ref, *rest):
    out_ref, ys_ref, xa_ref, xb_ref = rest[-4:]
    @pl.when(pl.program_id(0) == 0)
    def _():
        spectrum_in(ys_ref, gy_ref[...])
        interleaved(xa_ref, xb_ref, x_ref[...])

    for m in range(STEP):
        k = pl.program_id(0) * STEP + m
        at = pl.multiple_of(k * 2 * C, 8)
        xa = xa_ref[pl.ds(at, 2 * C), :]
        xb = xb_ref[pl.ds(at, 2 * C), :]
        for o in range(C):
            row = pl.ds(o * KB + k, 1)
            out_ref[m, o * 2 * C : (o + 1) * 2 * C, :] = ys_ref[0, row, :] * xa + ys_ref[1, row, :] * xb


def prep_body(skip_ref, up_ref, down_ref, ws_ref, wst_ref, w1_ref, w1t_ref, w2_ref, w2t_ref):
    def spread(rows):
        r = lax.broadcasted_iota(jnp.int32, (8 * rows, rows), 0) // 8
        c = lax.broadcasted_iota(jnp.int32, (8 * rows, rows), 1)
        return jnp.where(r == c, 1.0, 0.0).astype(BF)

    wide = {n: spread(n) for n in (C, F)}

    def same(rows, cols):
        r = lax.broadcasted_iota(jnp.int32, (8 * rows, 8 * cols), 0) % 8
        c = lax.broadcasted_iota(jnp.int32, (8 * rows, 8 * cols), 1) % 8
        return r == c

    masks = {(a, b): same(a, b) for a, b in ((C, C), (F, C), (C, F))}

    def expand(weight, a, b, straight_ref, turned_ref, layer):
        rows = dot(wide[a], weight).astype(BF)
        full = dot_nt(rows, wide[b])
        straight_ref[layer] = jnp.where(masks[a, b], full, 0.0).astype(BF)
        cols = dot_nt(wide[b], weight).astype(BF)
        full = dot_nt(cols, wide[a])
        turned_ref[layer] = jnp.where(masks[b, a], full, 0.0).astype(BF)

    for layer in range(LAYERS):
        expand(skip_ref[layer], C, C, ws_ref, wst_ref, layer)
        expand(up_ref[layer], F, C, w1_ref, w1t_ref, layer)
        expand(down_ref[layer], C, F, w2_ref, w2t_ref, layer)


FIELD = (CP, 2, ROWS, N)
LIMIT = pltpu.CompilerParams(vmem_limit_bytes=60 * 1024 * 1024)


def full(shape):
    zeros = (0,) * len(shape)
    return pl.BlockSpec(tuple(shape), lambda *_: zeros)


def part(shape, index):
    return pl.BlockSpec(tuple(shape), lambda *_: tuple(index))


def wire_part(slot, rows=WIRE):
    return part((SLABS, rows, LANES), (0, slot, 0))


def layer_part(shape, layer):
    return part((None,) + tuple(shape), (layer,) + (0,) * len(shape))


def spec_part(layer):
    return part((None, KB, 2 * C * C, LANES), (layer, 0, 0, 0))


def shape_of(shape, dtype):
    return jax.ShapeDtypeStruct(tuple(shape), dtype)


def call(body, name, args, outs, scratch=(), into=None):
    arrays = [a for a, _ in args]
    specs = [s for _, s in args]
    aliases = {}
    if into is not None:
        aliases = {len(arrays): into[0]}
        arrays.append(into[1])
        specs.append(pl.BlockSpec(memory_space=pl.ANY))
        inner, count = body, len(arrays)

        def body(*refs):
            inner(*refs[: count - 1], *refs[count:])

    return pl.pallas_call(
        body,
        out_shape=[o for o, _ in outs],
        grid_spec=pltpu.PrefetchScalarGridSpec(
            num_scalar_prefetch=0,
            grid=(1,),
            in_specs=specs,
            out_specs=[s for _, s in outs],
            scratch_shapes=list(scratch),
        ),
        input_output_aliases=aliases,
        compiler_params=LIMIT,
        name=name,
    )(*arrays)


FIELD_OUT = (shape_of(FIELD, BF), full(FIELD))
LEFT = pltpu.VMEM((CP * ROWS, 4 * M), BF)


def row_dft(field, tabs, slot, slots, into=None):
    out = (shape_of((SLABS, slots * WIRE, LANES), BF), wire_part(slot))
    return call(
        row_dft_body,
        "row_dft",
        [(field, full(FIELD)), (tabs["ew"], full((2 * M, N)))],
        [out],
        into=None if into is None else (0, into),
    )[0]


def forward_rows(wire, slot, field, kron, layer, tabs, keep, last, send_slot=0, slots=1, into=None):
    outs = [FIELD_OUT]
    if not last:
        outs.append((shape_of((SLABS, slots * WIRE, LANES), BF), wire_part(send_slot)))
    if keep:
        outs += [FIELD_OUT, FIELD_OUT]
    return call(
        functools.partial(forward_body, keep, last, len(field)),
        "forward_rows",
        [(f, full(f.shape)) for f in field]
        + [
            (wire, wire_part(slot)),
            (kron["ws"], layer_part((8 * C, 8 * C), layer)),
            (kron["w1"], layer_part((8 * F, 8 * C), layer)),
            (kron["w2"], layer_part((8 * C, 8 * F), layer)),
            (tabs["eiz"], full((2, 4 * M, N))),
            (tabs["ew"], full((2 * M, N))),
        ],
        outs,
        scratch=[LEFT, pltpu.VMEM(FIELD, F32)],
        into=None if into is None else (1, into),
    )


def back_rows(first, layer, wire, field, kron, tabs, slots, into, top=None, base=None, grads=None, y=None, slope=None):
    args = [(f, full(f.shape)) for f in field] + [
        (wire, wire_part(0)),
        (tabs["eiz" if first else "ewz"], full((2, 4 * M, N))),
        (kron["wst"], layer_part((8 * C, 8 * C), layer)),
        (kron["w1"], layer_part((8 * F, 8 * C), layer)),
        (kron["w1t"], layer_part((8 * C, 8 * F), layer)),
        (kron["w2t"], layer_part((8 * F, 8 * C), layer)),
        (tabs["ei"], full((2 * M, N))),
    ]
    if first:
        args += [(top, full(FIELD)), (kron["ws"], layer_part((8 * C, 8 * C), layer))]
    else:
        args += [(base, full(FIELD)), (grads, full((F, LANES))), (y, full(FIELD)), (slope, full(FIELD))]
    scratch = [
        pltpu.VMEM(FIELD, BF),
        pltpu.VMEM((8 * F, 8 * C), F32),
        pltpu.VMEM((8 * F, 8 * C), F32),
        pltpu.VMEM((8 * C, 8 * C), F32),
        LEFT,
        pltpu.VMEM(FIELD, F32 if first else BF),
    ]
    return call(
        functools.partial(back_body, first, layer, len(field)),
        "back_rows",
        args,
        [
            FIELD_OUT,
            (shape_of((SLABS, slots * WIRE, LANES), BF), wire_part(0)),
            (shape_of((F, LANES), F32), full((F, LANES))),
        ],
        scratch=scratch,
        into=None if into is None else (1, into),
    )


SPECTRUM = (WIRE, 4 * M)
SPECTRUM_OUT = (shape_of(SPECTRUM, BF), full(SPECTRUM))
HALF = pltpu.VMEM((2, WIRE, LANES), F32)
MIXED = pltpu.VMEM((2 * WIRE, LANES), F32)
COL = (SLABS, 2 * ROWS, 4 * M)


def spectrum(wire, slot, tabs):
    return call(
        spectrum_body, "spectrum", [(wire, wire_part(slot)), (tabs["col"], full(COL))], [SPECTRUM_OUT]
    )[0]


def mix_out(x, spec, layer, tabs, slot, slots, into=None):
    return call(
        mix_body,
        "mix_out",
        [(x, full(SPECTRUM)), (spec, spec_part(layer)), (tabs["col"], full(COL))],
        [(shape_of((SLABS, slots * WIRE, LANES), BF), wire_part(slot))],
        scratch=[MIXED, MIXED, HALF],
        into=None if into is None else (0, into),
    )[0]


def modes(wire, slot, spec, layer, tabs, send_slot, slots, into=None):
    return call(
        modes_body,
        "modes",
        [(wire, wire_part(slot)), (spec, spec_part(layer)), (tabs["col"], full(COL))],
        [SPECTRUM_OUT, (shape_of((SLABS, slots * WIRE, LANES), BF), wire_part(send_slot))],
        scratch=[MIXED, MIXED, HALF],
        into=None if into is None else (1, into),
    )


def modes_back(wire, spec, layer, tabs, grads=None, slots=1, into=None):
    tail = grads is not None
    rows = WIRE + (F if tail else 0)
    args = [(wire, wire_part(0)), (spec, spec_part(layer)), (tabs["col"], full(COL))]
    if tail:
        args.append((grads, full((F, LANES))))
    return call(
        functools.partial(modes_back_body, tail),
        "modes_back",
        args,
        [(shape_of((SLABS, slots * rows, LANES), BF), wire_part(0, rows)), SPECTRUM_OUT],
        scratch=[MIXED, MIXED, HALF, HALF],
        into=None if into is None else (0, into),
    )


def spec_grad(gy, x, layer, into=None):
    args, specs, aliases = [gy, x], [full(SPECTRUM), full(SPECTRUM)], {}
    body = spec_grad_body
    if into is not None:
        args.append(into)
        specs.append(pl.BlockSpec(memory_space=pl.ANY))
        aliases = {2: 0}
    return pl.pallas_call(
        body,
        out_shape=shape_of((LAYERS, KB, 2 * C * C, LANES), F32),
        grid_spec=pltpu.PrefetchScalarGridSpec(
            num_scalar_prefetch=0,
            grid=(KB // STEP,),
            in_specs=specs,
            out_specs=pl.BlockSpec(
                (None, STEP, 2 * C * C, LANES), lambda k: (layer, k, 0, 0)
            ),
            scratch_shapes=[HALF, MIXED, MIXED],
        ),
        input_output_aliases=aliases,
        compiler_params=LIMIT,
        name="spec_grad",
    )(*args)


def finish(wire, base, tabs):
    rows = WIRE + F
    return call(
        finish_body,
        "finish",
        [(wire, wire_part(0, rows)), (base, full(FIELD)), (tabs["ewz"], full((2, 4 * M, N)))],
        [FIELD_OUT] + [(shape_of((2 * C, n), F32), full((2 * C, n))) for n in (F, F, C)],
        scratch=[LEFT],
    )


def prep(skip_w, up_w, down_w):
    names = ["ws", "wst", "w1", "w1t", "w2", "w2t"]
    sizes = [(C, C), (C, C), (F, C), (C, F), (C, F), (F, C)]
    outs = [(LAYERS, 8 * a, 8 * b) for a, b in sizes]
    res = call(
        prep_body,
        "prep",
        [(w, part((None,) + w.shape[1:], (0,) * w.ndim)) for w in (skip_w, up_w, down_w)],
        [(shape_of(o, BF), full(o)) for o in outs],
    )
    return dict(zip(names, res))


def exchange(wire):
    return lax.all_to_all(wire, "slab", split_axis=0, concat_axis=0, tiled=True)


def shifted(block, distance):
    count = lax.axis_size("section")
    return lax.ppermute(block, "section", [(i, (i + distance) % count) for i in range(count)])


def shards(emitted, returned, stash, skip_w, up_w, down_w, spec_w):
    tabs = {name: jnp.asarray(value) for name, value in np_tables().items()}
    half = lax.axis_size("section") // 2
    emitted = emitted.reshape(FIELD)
    returned = returned.reshape(FIELD)
    stash = stash.reshape(FIELD)
    spec_w = spec_w[0].transpose(0, 1, 3, 4, 2, 5).reshape(LAYERS, KB, 2 * C * C, LANES)
    together = lax.optimization_barrier
    kept_a = shifted(stash[: CUTS[0]], half)
    kron = prep(skip_w, up_w, down_w)
    wire = row_dft(stash, tabs, 0, 2)
    wire = row_dft(emitted, tabs, 1, 2, into=wire)
    wire, kept_a, kron, stash_b = together((wire, kept_a, kron, stash[CUTS[0] : CUTS[1]]))
    wire = exchange(wire)
    kept_b = shifted(stash_b, half)
    x_0 = shifted(spectrum(wire, 0, tabs), half)
    ahead_x = shifted(spectrum(wire, 1, tabs), 1)
    stash_c, x_0, kept_b = together((stash[CUTS[1] :], x_0, kept_b))
    kept_c = shifted(stash_c, half)

    wire = mix_out(x_0, spec_w, 0, tabs, 0, 1)
    kept_c, wire, ahead_x = together((kept_c, wire, ahead_x))
    wire = exchange(wire)
    kept = (kept_a, kept_b, kept_c)
    out = mix_out(ahead_x, spec_w, 0, tabs, 1, 2)
    emitted, returned, wire, out = together((emitted, returned, wire, out))
    ahead = shifted(emitted, 1)
    top = shifted(returned, -1)
    kept_1, out, y_0, slope_0 = forward_rows(wire, 0, kept, kron, 0, tabs, True, False, 0, 2, into=out)
    second = exchange(out)
    x_1, out = modes(second, 0, spec_w, 1, tabs, 0, 1)
    wire = exchange(out)
    ahead_1, out = forward_rows(second, 1, (ahead,), kron, 0, tabs, False, False, 1, 2)
    wire, ahead_1, out = together((wire, ahead_1, out))

    base, out, grads = back_rows(True, 1, wire, (kept_1,), kron, tabs, 2, out, top=top)
    third = exchange(out)
    out, gy_1 = modes_back(third, spec_w, 1, tabs)
    wire = exchange(out)
    _, out = modes(third, 1, spec_w, 1, tabs, 1, 2)
    wire, out = together((wire, out))
    base, out, grads = back_rows(
        False, 0, wire, kept, kron, tabs, 2, out, base=base, grads=grads, y=y_0, slope=slope_0
    )
    fourth = exchange(out)
    grad_spec = spec_grad(gy_1, x_1, 1)
    fourth, grad_spec = together((fourth, grad_spec))
    out, gy_0 = modes_back(fourth, spec_w, 0, tabs, grads)
    wire = exchange(out)
    grad_spec = spec_grad(gy_0, x_0, 0, into=grad_spec)
    (sent,) = forward_rows(fourth, 1, (ahead_1,), kron, 1, tabs, False, True)
    wire, grad_spec, sent = together((wire, grad_spec, sent))
    back_grad, grad_down, grad_up, grad_skip = finish(wire, base, tabs)
    grad_skip = grad_skip.reshape(C, LAYERS, C).transpose(1, 0, 2)
    grad_up = grad_up.reshape(C, LAYERS, F).transpose(1, 2, 0)
    grad_down = grad_down.reshape(C, LAYERS, F).transpose(1, 0, 2)
    field = (1, C, ROWS, N)
    return (
        sent.reshape(field),
        back_grad.reshape(field),
        grad_skip[None],
        grad_up[None],
        grad_down[None],
        grad_spec.reshape(LAYERS, KB, C, C, 2, LANES).transpose(0, 1, 4, 2, 3, 5)[None],
    )


def solution(mesh):
    field = P("section", None, "slab", None)
    weight = P("section", None, None, None)
    spec = P("section", None, "slab", None, None, None, None)
    return jax.shard_map(
        shards,
        mesh=mesh,
        in_specs=(field, field, field, weight, weight, weight, spec),
        out_specs=(field, field, weight, weight, weight, spec),
        check_vma=False,
    )
```

```python
import functools

import jax
import jax.numpy as jnp
import numpy as np
import ml_dtypes
from jax import lax
from jax.experimental import pallas as pl
from jax.experimental.pallas import tpu as pltpu
from jax.sharding import PartitionSpec as P

M = 64
LAYERS = 2
N = 512
C = 20
F = 80
SLABS = 8
ROWS = N // SLABS
KB = M // SLABS
CP = C // 2
STEP = 4
CUTS = (CP // 2, CP * 4 // 5)
WIRE = C * KB
LANES = 128
BF = jnp.bfloat16
F32 = jnp.float32

root_two_pi = 0.7978845608028654
cubic_coef = 0.044715


def np_angles(left_idx, right_idx, length):
    product_idx = left_idx[:, None] * right_idx[None, :] % length
    return np.float32(2.0 * np.pi / length) * product_idx.astype(np.float32)


def np_tables():
    cell = np.arange(N)
    low = np.arange(M)
    both = np.concatenate([low, low + (N - M)])
    along_w = np_angles(cell, low, N)
    cos_w, sin_w = np.cos(along_w), np.sin(along_w)
    row = np.stack([cos_w.T, -sin_w.T], 0)
    weight = np.where(low == 0, 1.0, 2.0).astype(np.float32)[None, :, None]
    back = row * weight
    along_h = np_angles(cell, both, N)
    cos_h, sin_h = np.cos(along_h), np.sin(along_h)
    col = np.stack([np.stack([cos_h, -sin_h], 1), np.stack([sin_h, cos_h], 1)], 0)
    col = col.reshape(2, SLABS, ROWS, 2, 2 * M).transpose(1, 0, 2, 3, 4).reshape(SLABS, 2 * ROWS, 4 * M)

    def forward(table, scale):
        t = table.reshape(2, SLABS, KB, N).transpose(1, 0, 2, 3).reshape(2 * M, N)
        return (t.astype(ml_dtypes.bfloat16).astype(np.float32) * scale).astype(ml_dtypes.bfloat16)

    def inverse(table, scale):
        t = table.reshape(2, SLABS, KB, N)
        out = np.zeros((2, 2, SLABS, 2, KB, N), np.float32)
        for c in range(2):
            out[c, :, :, c] = t
        out = out.reshape(2, 4 * M, N)
        return (out.astype(ml_dtypes.bfloat16).astype(np.float32) * scale).astype(ml_dtypes.bfloat16)

    return {
        "ew": forward(row, 1.0),
        "ei": forward(back, 1.0 / N),
        "ewz": inverse(row, 1.0),
        "eiz": inverse(back, 1.0 / N),
        "col": col.astype(ml_dtypes.bfloat16),
    }


def dot(a, b):
    return jnp.dot(a, b, preferred_element_type=F32)


def dot_nt(a, b):
    return lax.dot_general(a, b, (((1,), (1,)), ((), ())), preferred_element_type=F32)


def gate(t):
    t = t.astype(BF)
    u = t * (BF(root_two_pi) + BF(root_two_pi * cubic_coef) * (t * t))
    half = BF(0.5) * t
    return half + half * jnp.tanh(u)


def gate_and_slope(t):
    t = t.astype(BF)
    tt = t * t
    th = jnp.tanh(t * (BF(root_two_pi) + BF(root_two_pi * cubic_coef) * tt))
    half = BF(0.5) * t
    value = half + half * th
    slope = (BF(0.5) + BF(0.5) * th) + half * (BF(1.0) - th * th) * (
        BF(root_two_pi) + BF(3.0 * root_two_pi * cubic_coef) * tt
    )
    return value, slope


def rows_to_wire(read, table_ref, send_ref):
    lane = lax.broadcasted_iota(jnp.int32, (M, LANES), 1)
    low = lane < ROWS
    table = table_ref[...]
    for cp in range(0, CP, 2):
        res = dot_nt(table, read(cp, 2))
        for s in range(2):
            r = res[:, s * LANES : (s + 1) * LANES].reshape(SLABS, 2, KB, LANES)
            a = r[:, 0].reshape(M, LANES)
            b = r[:, 1].reshape(M, LANES)
            lo = jnp.where(low, a, pltpu.roll(b, ROWS, 1)).reshape(SLABS, 1, KB, LANES)
            hi = jnp.where(low, pltpu.roll(a, ROWS, 1), b).reshape(SLABS, 1, KB, LANES)
            out = jnp.concatenate([lo, hi], axis=1).reshape(SLABS, 2 * KB, LANES).astype(BF)
            at = (cp + s) * 2 * KB
            send_ref[:, at : at + 2 * KB, :] = out


def wire_to_rows(recv_ref, left_ref):
    for cp in range(CP):
        m = recv_ref[:, cp * 2 * KB : (cp + 1) * 2 * KB, :].reshape(2 * M, LANES)
        t = m.astype(F32).T.astype(BF)
        left_ref[cp * ROWS : (cp + 1) * ROWS, 0 : 2 * M] = t[:ROWS]
        left_ref[cp * ROWS : (cp + 1) * ROWS, 2 * M : 4 * M] = t[ROWS:]


def wide(block):
    x = block.astype(F32)
    return jnp.concatenate([x[:, :, s * 8 : s * 8 + 8, :].reshape(8 * C, N) for s in range(2)], axis=1)


def both(refs, where):
    blocks = [ref[where] for ref in refs]
    return blocks[0] if len(blocks) == 1 else jnp.concatenate(blocks, axis=0)


def narrow(x):
    parts = [x[:, s * N : (s + 1) * N].reshape(CP, 2, 8, N) for s in range(2)]
    return jnp.concatenate(parts, axis=2).astype(BF)


def field_read(ref):
    def read(cp, pairs):
        return ref[cp : cp + pairs].reshape(pairs * 2 * ROWS, N)

    return read


def row_dft_body(v_ref, table_ref, *rest):
    send_ref = rest[-1]
    rows_to_wire(field_read(v_ref), table_ref, send_ref)


def forward_body(keep, last, parts, *refs):
    v_refs, refs = refs[:parts], refs[parts:]
    u_ref, ws_ref, w1_ref, w2_ref, eiz_ref, ew_ref = refs[:6]
    outs = list(refs[6:])
    left_ref, z_ref = outs[-2:]
    outs = outs[:-2]
    out_ref = outs[0]
    at = 1
    if not last:
        send_ref = outs[at]
        at += 1
    if keep:
        y_ref, slope_ref = outs[at : at + 2]
    wire_to_rows(u_ref, left_ref)
    for c2 in range(2):
        z_ref[:, c2] = dot(left_ref[...], eiz_ref[c2]).reshape(CP, ROWS, N)

    def step(i, carry):
        h0 = pl.multiple_of(i * 16, 16)
        where = (slice(None), slice(None), pl.ds(h0, 16))
        v = wide(both(v_refs, where))
        z = wide(z_ref[where]) + dot(ws_ref[...], v.astype(BF))
        if keep:
            y, slope = gate_and_slope(z)
            y_ref[where] = narrow(y.astype(F32))
            slope_ref[where] = narrow(slope.astype(F32))
        else:
            y = gate(z)
        hidden = dot(w1_ref[...], y.astype(BF))
        out_ref[where] = narrow(v + dot(w2_ref[...], gate(hidden)))
        return carry

    lax.fori_loop(0, ROWS // 16, step, 0)
    if not last:
        rows_to_wire(field_read(out_ref), ew_ref, send_ref)


def back_body(first, layer, parts, *refs):
    v_refs, refs = refs[:parts], refs[parts:]
    u_ref, table_ref, wst_ref, w1_ref, w1t_ref, w2t_ref, ei_ref = refs[:7]
    if first:
        g_ref, ws_ref = refs[7:9]
        refs = refs[9:]
    else:
        base_in_ref, grads_in_ref, y_ref, slope_ref = refs[7:11]
        refs = refs[11:]
    base_ref, send_ref, grads_ref, gz_ref, gd_ref, gu_ref, gs_ref, left_ref, field_ref = refs
    wire_to_rows(u_ref, left_ref)
    for c2 in range(2):
        r = dot(left_ref[...], table_ref[c2]).reshape(CP, ROWS, N)
        if not first:
            r = (base_in_ref[:, c2].astype(F32) + r).astype(BF)
        field_ref[:, c2] = r
    if not first:
        g_ref = field_ref
    gd_ref[...] = jnp.zeros_like(gd_ref)
    gu_ref[...] = jnp.zeros_like(gu_ref)
    gs_ref[...] = jnp.zeros_like(gs_ref)

    def step(i, carry):
        h0 = pl.multiple_of(i * 16, 16)
        where = (slice(None), slice(None), pl.ds(h0, 16))
        g = wide(g_ref[where])
        gb = g.astype(BF)
        v = wide(both(v_refs, where)).astype(BF)
        if first:
            y, out_slope = gate_and_slope(wide(field_ref[where]) + dot(ws_ref[...], v))
            out_slope = out_slope.astype(F32)
        else:
            y = wide(y_ref[where]).astype(BF)
            out_slope = wide(slope_ref[where])
        act, slope = gate_and_slope(dot(w1_ref[...], y))
        gh = dot(w2t_ref[...], gb).astype(BF) * slope
        gz = (dot(w1t_ref[...], gh) * out_slope).astype(BF)
        base_ref[where] = narrow(g + dot(wst_ref[...], gz))
        gz_ref[where] = narrow(gz.astype(F32))
        gd_ref[...] += dot_nt(act.astype(BF), gb)
        gu_ref[...] += dot_nt(gh, y)
        gs_ref[...] += dot_nt(v, gz)
        return carry

    lax.fori_loop(0, ROWS // 16, step, 0)
    rows_to_wire(field_read(gz_ref), ei_ref, send_ref)
    total = jnp.zeros((F, LANES), F32) if first else grads_in_ref[...]
    for ref, slot in ((gd_ref, 0), (gu_ref, 1), (gs_ref, 2)):
        rows, cols = ref.shape
        r_idx = lax.broadcasted_iota(jnp.int32, (rows, cols), 0) % 8
        c_idx = lax.broadcasted_iota(jnp.int32, (rows, cols), 1) % 8
        kept = jnp.where(r_idx == c_idx, ref[...], 0.0).reshape(rows // 8, 8, cols)
        summed = jnp.sum(kept, axis=1)
        offset = slot * 2 * C + layer
        pick_r = lax.broadcasted_iota(jnp.int32, (cols, LANES), 0) // 8 * 2 + offset
        pick_c = lax.broadcasted_iota(jnp.int32, (cols, LANES), 1)
        pick = jnp.where(pick_r == pick_c, 1.0 / N, 0.0).astype(F32)
        placed = jnp.dot(summed, pick, precision=lax.Precision.HIGHEST, preferred_element_type=F32)
        if rows // 8 < F:
            placed = jnp.concatenate([placed, jnp.zeros((F - rows // 8, LANES), F32)], axis=0)
        total = total + placed
    grads_ref[...] = total


def finish_body(recv_ref, base_ref, ewz_ref, out_ref, down_ref, up_ref, skip_ref, left_ref):
    wire_to_rows(recv_ref, left_ref)
    for c2 in range(2):
        r = dot(left_ref[...], ewz_ref[c2]).reshape(CP, ROWS, N)
        out_ref[:, c2] = (base_ref[:, c2].astype(F32) + r).astype(BF)
    grads = jnp.sum(recv_ref[:, WIRE : WIRE + F, :].astype(F32), axis=0).T
    down_ref[...] = grads[: 2 * C]
    up_ref[...] = grads[2 * C : 4 * C]
    skip_ref[...] = grads[4 * C : 6 * C, :C]


def to_spectrum(recv_ref, col_ref):
    total = jnp.zeros((WIRE, 4 * M), F32)
    for j in range(0, SLABS, 2):
        pair = jnp.concatenate([recv_ref[j], recv_ref[j + 1]], axis=1)
        total = total + dot(pair, col_ref[j : j + 2].reshape(4 * ROWS, 4 * M))
    return total


def from_spectrum(values, col_ref, send_ref, scale):
    for j in range(0, SLABS, 2):
        r = dot_nt(values, col_ref[j : j + 2].reshape(4 * ROWS, 4 * M))
        if scale != 1.0:
            r = r * scale
        r = r.astype(BF)
        send_ref[j, 0:WIRE, :] = r[:, :LANES]
        send_ref[j + 1, 0:WIRE, :] = r[:, LANES:]


def spectrum_in(ref, value):
    value = value.astype(F32)
    ref[0] = value[:, :LANES]
    ref[1] = value[:, LANES:]


def spectrum_of(ref):
    return jnp.concatenate([ref[0], ref[1]], axis=1).astype(BF)


def interleaved(xa_ref, xb_ref, value):
    value = value.astype(F32)
    re = value[:, :LANES].reshape(C, KB, LANES)
    im = value[:, LANES:].reshape(C, KB, LANES)
    for c in range(C):
        xa_ref[pl.ds(2 * c, KB, stride=2 * C), :] = re[c]
        xa_ref[pl.ds(2 * c + 1, KB, stride=2 * C), :] = -im[c]
        xb_ref[pl.ds(2 * c, KB, stride=2 * C), :] = im[c]
        xb_ref[pl.ds(2 * c + 1, KB, stride=2 * C), :] = re[c]


def mix(spec_ref, xa_ref, xb_ref, y_ref):
    def one(k, carry):
        at = pl.multiple_of(k * 2 * C, 8)
        xa = xa_ref[pl.ds(at, 2 * C), :]
        xb = xb_ref[pl.ds(at, 2 * C), :]
        for o in range(0, C, 2):
            w = spec_ref[k, o * 2 * C : (o + 2) * 2 * C, :].astype(F32)
            for s in range(2):
                r = w[s * 2 * C : (s + 1) * 2 * C]
                row = pl.ds((o + s) * KB + k, 1)
                y_ref[0, row, :] = jnp.sum(r * xa, axis=0, keepdims=True)
                y_ref[1, row, :] = jnp.sum(r * xb, axis=0, keepdims=True)
        return carry

    lax.fori_loop(0, KB, one, 0)


def spectrum_body(recv_ref, col_ref, x_ref):
    x_ref[...] = (to_spectrum(recv_ref, col_ref) * (1.0 / N)).astype(BF)


def mix_body(x_ref, spec_ref, col_ref, *rest):
    send_ref, xa_ref, xb_ref, ys_ref = rest[-4:]
    interleaved(xa_ref, xb_ref, x_ref[...])
    mix(spec_ref, xa_ref, xb_ref, ys_ref)
    from_spectrum(spectrum_of(ys_ref), col_ref, send_ref, 1.0)


def modes_body(recv_ref, spec_ref, col_ref, *rest):
    x_ref, send_ref, xa_ref, xb_ref, ys_ref = rest[-5:]
    x = (to_spectrum(recv_ref, col_ref) * (1.0 / N)).astype(BF)
    x_ref[...] = x
    interleaved(xa_ref, xb_ref, x)
    mix(spec_ref, xa_ref, xb_ref, ys_ref)
    from_spectrum(spectrum_of(ys_ref), col_ref, send_ref, 1.0)


def modes_back_body(tail, *refs):
    refs = list(refs)
    recv_ref, spec_ref, col_ref = refs[:3]
    refs = refs[3:]
    if tail:
        grads_ref = refs.pop(0)
    send_ref, gy_ref, ga_ref, gb_ref, ys_ref, gx_ref = refs
    gy = to_spectrum(recv_ref, col_ref).astype(BF)
    gy_ref[...] = gy
    spectrum_in(ys_ref, gy)

    def one(k, carry):
        acc_a = jnp.zeros((2 * C, LANES), F32)
        acc_b = jnp.zeros((2 * C, LANES), F32)
        for o in range(0, C, 2):
            w = spec_ref[k, o * 2 * C : (o + 2) * 2 * C, :].astype(F32)
            for s in range(2):
                r = w[s * 2 * C : (s + 1) * 2 * C]
                row = pl.ds((o + s) * KB + k, 1)
                acc_a = acc_a + r * ys_ref[0, row, :]
                acc_b = acc_b + r * ys_ref[1, row, :]
        at = pl.multiple_of(k * 2 * C, 8)
        ga_ref[pl.ds(at, 2 * C), :] = acc_a
        gb_ref[pl.ds(at, 2 * C), :] = acc_b
        return carry

    lax.fori_loop(0, KB, one, 0)
    for c in range(C):
        re = pl.ds(2 * c, KB, stride=2 * C)
        im = pl.ds(2 * c + 1, KB, stride=2 * C)
        gx_ref[0, c * KB : (c + 1) * KB, :] = ga_ref[re, :] + gb_ref[im, :]
        gx_ref[1, c * KB : (c + 1) * KB, :] = gb_ref[re, :] - ga_ref[im, :]
    from_spectrum(spectrum_of(gx_ref), col_ref, send_ref, 1.0 / N)
    if tail:
        g = grads_ref[...].astype(BF)
        for j in range(SLABS):
            send_ref[j, WIRE : WIRE + F, :] = g


def spec_grad_body(gy_ref, x_ref, *rest):
    out_ref, ys_ref, xa_ref, xb_ref = rest[-4:]
    @pl.when(pl.program_id(0) == 0)
    def _():
        spectrum_in(ys_ref, gy_ref[...])
        interleaved(xa_ref, xb_ref, x_ref[...])

    for m in range(STEP):
        k = pl.program_id(0) * STEP + m
        at = pl.multiple_of(k * 2 * C, 8)
        xa = xa_ref[pl.ds(at, 2 * C), :]
        xb = xb_ref[pl.ds(at, 2 * C), :]
        for o in range(C):
            row = pl.ds(o * KB + k, 1)
            out_ref[m, o * 2 * C : (o + 1) * 2 * C, :] = ys_ref[0, row, :] * xa + ys_ref[1, row, :] * xb


def prep_body(skip_ref, up_ref, down_ref, ws_ref, wst_ref, w1_ref, w1t_ref, w2_ref, w2t_ref):
    def spread(rows):
        r = lax.broadcasted_iota(jnp.int32, (8 * rows, rows), 0) // 8
        c = lax.broadcasted_iota(jnp.int32, (8 * rows, rows), 1)
        return jnp.where(r == c, 1.0, 0.0).astype(BF)

    wide = {n: spread(n) for n in (C, F)}

    def same(rows, cols):
        r = lax.broadcasted_iota(jnp.int32, (8 * rows, 8 * cols), 0) % 8
        c = lax.broadcasted_iota(jnp.int32, (8 * rows, 8 * cols), 1) % 8
        return r == c

    masks = {(a, b): same(a, b) for a, b in ((C, C), (F, C), (C, F))}

    def expand(weight, a, b, straight_ref, turned_ref, layer):
        rows = dot(wide[a], weight).astype(BF)
        full = dot_nt(rows, wide[b])
        straight_ref[layer] = jnp.where(masks[a, b], full, 0.0).astype(BF)
        cols = dot_nt(wide[b], weight).astype(BF)
        full = dot_nt(cols, wide[a])
        turned_ref[layer] = jnp.where(masks[b, a], full, 0.0).astype(BF)

    for layer in range(LAYERS):
        expand(skip_ref[layer], C, C, ws_ref, wst_ref, layer)
        expand(up_ref[layer], F, C, w1_ref, w1t_ref, layer)
        expand(down_ref[layer], C, F, w2_ref, w2t_ref, layer)


FIELD = (CP, 2, ROWS, N)
MIB = 1024 * 1024
LIMIT = pltpu.CompilerParams(vmem_limit_bytes=60 * MIB)


def full(shape):
    zeros = (0,) * len(shape)
    return pl.BlockSpec(tuple(shape), lambda *_: zeros)


def part(shape, index):
    return pl.BlockSpec(tuple(shape), lambda *_: tuple(index))


def wire_part(slot, rows=WIRE):
    return part((SLABS, rows, LANES), (0, slot, 0))


def layer_part(shape, layer):
    return part((None,) + tuple(shape), (layer,) + (0,) * len(shape))


def spec_part(layer):
    return part((None, KB, 2 * C * C, LANES), (layer, 0, 0, 0))


def shape_of(shape, dtype):
    return jax.ShapeDtypeStruct(tuple(shape), dtype)


def call(body, name, args, outs, scratch=(), into=None):
    arrays = [a for a, _ in args]
    specs = [s for _, s in args]
    aliases = {}
    if into is not None:
        aliases = {len(arrays): into[0]}
        arrays.append(into[1])
        specs.append(pl.BlockSpec(memory_space=pl.ANY))
        inner, count = body, len(arrays)

        def body(*refs):
            inner(*refs[: count - 1], *refs[count:])

    return pl.pallas_call(
        body,
        out_shape=[o for o, _ in outs],
        grid_spec=pltpu.PrefetchScalarGridSpec(
            num_scalar_prefetch=0,
            grid=(1,),
            in_specs=specs,
            out_specs=[s for _, s in outs],
            scratch_shapes=list(scratch),
        ),
        input_output_aliases=aliases,
        compiler_params=LIMIT,
        name=name,
    )(*arrays)


FIELD_OUT = (shape_of(FIELD, BF), full(FIELD))
LEFT = pltpu.VMEM((CP * ROWS, 4 * M), BF)


def row_dft(field, tabs, slot, slots, into=None):
    out = (shape_of((SLABS, slots * WIRE, LANES), BF), wire_part(slot))
    return call(
        row_dft_body,
        "row_dft",
        [(field, full(FIELD)), (tabs["ew"], full((2 * M, N)))],
        [out],
        into=None if into is None else (0, into),
    )[0]


def forward_rows(wire, slot, field, kron, layer, tabs, keep, last, send_slot=0, slots=1, into=None):
    outs = [FIELD_OUT]
    if not last:
        outs.append((shape_of((SLABS, slots * WIRE, LANES), BF), wire_part(send_slot)))
    if keep:
        outs += [FIELD_OUT, FIELD_OUT]
    return call(
        functools.partial(forward_body, keep, last, len(field)),
        "forward_rows",
        [(f, full(f.shape)) for f in field]
        + [
            (wire, wire_part(slot)),
            (kron["ws"], layer_part((8 * C, 8 * C), layer)),
            (kron["w1"], layer_part((8 * F, 8 * C), layer)),
            (kron["w2"], layer_part((8 * C, 8 * F), layer)),
            (tabs["eiz"], full((2, 4 * M, N))),
            (tabs["ew"], full((2 * M, N))),
        ],
        outs,
        scratch=[LEFT, pltpu.VMEM(FIELD, F32)],
        into=None if into is None else (1, into),
    )


def back_rows(first, layer, wire, field, kron, tabs, slots, into, top=None, base=None, grads=None, y=None, slope=None):
    args = [(f, full(f.shape)) for f in field] + [
        (wire, wire_part(0)),
        (tabs["eiz" if first else "ewz"], full((2, 4 * M, N))),
        (kron["wst"], layer_part((8 * C, 8 * C), layer)),
        (kron["w1"], layer_part((8 * F, 8 * C), layer)),
        (kron["w1t"], layer_part((8 * C, 8 * F), layer)),
        (kron["w2t"], layer_part((8 * F, 8 * C), layer)),
        (tabs["ei"], full((2 * M, N))),
    ]
    if first:
        args += [(top, full(FIELD)), (kron["ws"], layer_part((8 * C, 8 * C), layer))]
    else:
        args += [(base, full(FIELD)), (grads, full((F, LANES))), (y, full(FIELD)), (slope, full(FIELD))]
    scratch = [
        pltpu.VMEM(FIELD, BF),
        pltpu.VMEM((8 * F, 8 * C), F32),
        pltpu.VMEM((8 * F, 8 * C), F32),
        pltpu.VMEM((8 * C, 8 * C), F32),
        LEFT,
        pltpu.VMEM(FIELD, F32 if first else BF),
    ]
    return call(
        functools.partial(back_body, first, layer, len(field)),
        "back_rows",
        args,
        [
            FIELD_OUT,
            (shape_of((SLABS, slots * WIRE, LANES), BF), wire_part(0)),
            (shape_of((F, LANES), F32), full((F, LANES))),
        ],
        scratch=scratch,
        into=None if into is None else (1, into),
    )


SPECTRUM = (WIRE, 4 * M)
SPECTRUM_OUT = (shape_of(SPECTRUM, BF), full(SPECTRUM))
HALF = pltpu.VMEM((2, WIRE, LANES), F32)
MIXED = pltpu.VMEM((2 * WIRE, LANES), F32)
COL = (SLABS, 2 * ROWS, 4 * M)


def spectrum(wire, slot, tabs):
    return call(
        spectrum_body, "spectrum", [(wire, wire_part(slot)), (tabs["col"], full(COL))], [SPECTRUM_OUT]
    )[0]


def mix_out(x, spec, layer, tabs, slot, slots, into=None):
    return call(
        mix_body,
        "mix_out",
        [(x, full(SPECTRUM)), (spec, spec_part(layer)), (tabs["col"], full(COL))],
        [(shape_of((SLABS, slots * WIRE, LANES), BF), wire_part(slot))],
        scratch=[MIXED, MIXED, HALF],
        into=None if into is None else (0, into),
    )[0]


def modes(wire, slot, spec, layer, tabs, send_slot, slots, into=None):
    return call(
        modes_body,
        "modes",
        [(wire, wire_part(slot)), (spec, spec_part(layer)), (tabs["col"], full(COL))],
        [SPECTRUM_OUT, (shape_of((SLABS, slots * WIRE, LANES), BF), wire_part(send_slot))],
        scratch=[MIXED, MIXED, HALF],
        into=None if into is None else (1, into),
    )


def modes_back(wire, spec, layer, tabs, grads=None, slots=1, into=None):
    tail = grads is not None
    rows = WIRE + (F if tail else 0)
    args = [(wire, wire_part(0)), (spec, spec_part(layer)), (tabs["col"], full(COL))]
    if tail:
        args.append((grads, full((F, LANES))))
    return call(
        functools.partial(modes_back_body, tail),
        "modes_back",
        args,
        [(shape_of((SLABS, slots * rows, LANES), BF), wire_part(0, rows)), SPECTRUM_OUT],
        scratch=[MIXED, MIXED, HALF, HALF],
        into=None if into is None else (0, into),
    )


def spec_grad(gy, x, layer, into=None):
    args, specs, aliases = [gy, x], [full(SPECTRUM), full(SPECTRUM)], {}
    body = spec_grad_body
    if into is not None:
        args.append(into)
        specs.append(pl.BlockSpec(memory_space=pl.ANY))
        aliases = {2: 0}
    return pl.pallas_call(
        body,
        out_shape=shape_of((LAYERS, KB, 2 * C * C, LANES), F32),
        grid_spec=pltpu.PrefetchScalarGridSpec(
            num_scalar_prefetch=0,
            grid=(KB // STEP,),
            in_specs=specs,
            out_specs=pl.BlockSpec(
                (None, STEP, 2 * C * C, LANES), lambda k: (layer, k, 0, 0)
            ),
            scratch_shapes=[HALF, MIXED, MIXED],
        ),
        input_output_aliases=aliases,
        compiler_params=LIMIT,
        name="spec_grad",
    )(*args)


def finish(wire, base, tabs):
    rows = WIRE + F
    return call(
        finish_body,
        "finish",
        [(wire, wire_part(0, rows)), (base, full(FIELD)), (tabs["ewz"], full((2, 4 * M, N)))],
        [FIELD_OUT] + [(shape_of((2 * C, n), F32), full((2 * C, n))) for n in (F, F, C)],
        scratch=[LEFT],
    )


def prep(skip_w, up_w, down_w):
    names = ["ws", "wst", "w1", "w1t", "w2", "w2t"]
    sizes = [(C, C), (C, C), (F, C), (C, F), (C, F), (F, C)]
    outs = [(LAYERS, 8 * a, 8 * b) for a, b in sizes]
    res = call(
        prep_body,
        "prep",
        [(w, part((None,) + w.shape[1:], (0,) * w.ndim)) for w in (skip_w, up_w, down_w)],
        [(shape_of(o, BF), full(o)) for o in outs],
    )
    return dict(zip(names, res))


def exchange(wire):
    return lax.all_to_all(wire, "slab", split_axis=0, concat_axis=0, tiled=True)


def shifted(block, distance):
    count = lax.axis_size("section")
    return lax.ppermute(block, "section", [(i, (i + distance) % count) for i in range(count)])


def shards(emitted, returned, stash, skip_w, up_w, down_w, spec_w):
    tabs = {name: jnp.asarray(value) for name, value in np_tables().items()}
    half = lax.axis_size("section") // 2
    emitted = emitted.reshape(FIELD)
    returned = returned.reshape(FIELD)
    stash = stash.reshape(FIELD)
    spec_w = spec_w[0].transpose(0, 1, 3, 4, 2, 5).reshape(LAYERS, KB, 2 * C * C, LANES)
    together = lax.optimization_barrier
    kept_a = shifted(stash[: CUTS[0]], half)
    kron = prep(skip_w, up_w, down_w)
    wire = row_dft(stash, tabs, 0, 2)
    wire = row_dft(emitted, tabs, 1, 2, into=wire)
    wire, kept_a, kron, stash_b = together((wire, kept_a, kron, stash[CUTS[0] : CUTS[1]]))
    wire = exchange(wire)
    kept_b = shifted(stash_b, half)
    x_0 = shifted(spectrum(wire, 0, tabs), half)
    ahead_x = shifted(spectrum(wire, 1, tabs), 1)
    stash_c, x_0, kept_b = together((stash[CUTS[1] :], x_0, kept_b))
    kept_c = shifted(stash_c, half)

    wire = mix_out(x_0, spec_w, 0, tabs, 0, 1)
    kept_c, wire, ahead_x = together((kept_c, wire, ahead_x))
    wire = exchange(wire)
    kept = (kept_a, kept_b, kept_c)
    out = mix_out(ahead_x, spec_w, 0, tabs, 1, 2)
    emitted, returned, wire, out = together((emitted, returned, wire, out))
    ahead = shifted(emitted, 1)
    top = shifted(returned, -1)
    kept_1, out, y_0, slope_0 = forward_rows(wire, 0, kept, kron, 0, tabs, True, False, 0, 2, into=out)
    second = exchange(out)
    x_1, out = modes(second, 0, spec_w, 1, tabs, 0, 1)
    wire = exchange(out)
    ahead_1, out = forward_rows(second, 1, (ahead,), kron, 0, tabs, False, False, 1, 2)
    wire, ahead_1, out = together((wire, ahead_1, out))

    base, out, grads = back_rows(True, 1, wire, (kept_1,), kron, tabs, 2, out, top=top)
    third = exchange(out)
    out, gy_1 = modes_back(third, spec_w, 1, tabs)
    wire = exchange(out)
    _, out = modes(third, 1, spec_w, 1, tabs, 1, 2)
    wire, out = together((wire, out))
    base, out, grads = back_rows(
        False, 0, wire, kept, kron, tabs, 2, out, base=base, grads=grads, y=y_0, slope=slope_0
    )
    fourth = exchange(out)
    grad_spec = spec_grad(gy_1, x_1, 1)
    fourth, grad_spec = together((fourth, grad_spec))
    out, gy_0 = modes_back(fourth, spec_w, 0, tabs, grads)
    wire = exchange(out)
    grad_spec = spec_grad(gy_0, x_0, 0, into=grad_spec)
    (sent,) = forward_rows(fourth, 1, (ahead_1,), kron, 1, tabs, False, True)
    wire, grad_spec, sent = together((wire, grad_spec, sent))
    back_grad, grad_down, grad_up, grad_skip = finish(wire, base, tabs)
    grad_skip = grad_skip.reshape(C, LAYERS, C).transpose(1, 0, 2)
    grad_up = grad_up.reshape(C, LAYERS, F).transpose(1, 2, 0)
    grad_down = grad_down.reshape(C, LAYERS, F).transpose(1, 0, 2)
    field = (1, C, ROWS, N)
    return (
        sent.reshape(field),
        back_grad.reshape(field),
        grad_skip[None],
        grad_up[None],
        grad_down[None],
        grad_spec.reshape(LAYERS, KB, C, C, 2, LANES).transpose(0, 1, 4, 2, 3, 5)[None],
    )


def solution(mesh):
    field = P("section", None, "slab", None)
    weight = P("section", None, None, None)
    spec = P("section", None, "slab", None, None, None, None)
    return jax.shard_map(
        shards,
        mesh=mesh,
        in_specs=(field, field, field, weight, weight, weight, spec),
        out_specs=(field, field, weight, weight, weight, spec),
        check_vma=False,
    )
```
